256 devices in a mesh: rep: 4 (over x_lo, core), shard: 32 (over z, y), tp: 2 (over x_hi).
Axes of the slice: x: 4 (x_hi: 2, x_lo: 2; x = x_hi * 2 + x_lo), y: 4, z: 8, core: 2. Of those that a mesh axis runs over, the one named last changes fastest.
Arguments:
- expert_change: float32 [4, 4, 768, 3072], P('rep', None, 'shard', 'tp'), may hold values from -6 to 6
- table_change: float32 [4, 768, 16384], P('rep', 'shard', 'tp'), may hold values from -6 to 6
- expert_master: float32 [4, 3072, 768], P(None, 'shard'), may hold values from -6 to 6
- expert_moment: float32 [4, 3072, 768], P(None, 'shard'), may hold values from -6 to 6
- table_master: float32 [16384, 768], P('shard'), may hold values from -6 to 6
- table_moment: float32 [16384, 768], P('shard'), may hold values from -6 to 6
Outputs:
- expert_weights: float32 [4, 3072, 768], P(None, 'shard')
- expert_velocity: float32 [4, 3072, 768], P(None, 'shard')
- expert_copies: bfloat16 [4, 768, 3072], P(None, 'shard', 'tp')
- table_weights: float32 [16384, 768], P('shard')
- table_velocity: float32 [16384, 768], P('shard')
- table_copies: bfloat16 [768, 16384], P('shard', 'tp')
The draws below stay inside these ranges and needn't reach their ends.
All inputs are finite; a program needn't handle non-finite values.
Results may differ from the reference program's by a relative error of at most 0.001.
Values may be sent and summed in bfloat16 or wider, within the bound.
A program may use at most 128 MiB of HBM per device.

```python
import jax
import jax.numpy as jnp

D = 768
FF = 3072
VOCAB = 16384
MATS = 4
N_REP = 4


def level_of(key, dims, shards, low, largest):
    factor_of, own = 1.0, jax.random.fold_in(key, 6)
    for position, parts in shards:
        heights = jnp.exp(jax.random.uniform(jax.random.fold_in(own, position), (parts,), jnp.float32, low / len(shards), largest / len(shards)))
        factor_of = factor_of * jnp.repeat(heights, dims[position] // parts).reshape([-1 if axis == position else 1 for axis in range(len(dims))])
    return factor_of


def gaussian(rng, shape, spread, most, pieces=(), dtype=jnp.bfloat16):
    array = spread * jax.random.normal(rng, shape, jnp.float32)
    if pieces:
        array = array * level_of(rng, shape, pieces, -0.22, 0.18)
    return jnp.clip(array, -most, most).astype(dtype)


def setup_inputs(seed: int = 0) -> dict:
    splits = jax.random.split(jax.random.key(seed), 7)
    expert_change = gaussian(splits[0], (N_REP, MATS, D, FF), 1.0, 6.0, ((0, 4), (2, 32), (3, 2)), jnp.float32)
    table_change = gaussian(splits[1], (N_REP, D, VOCAB), 1.0, 6.0, ((0, 4), (1, 32), (2, 2)), jnp.float32)
    expert_master = gaussian(splits[2], (MATS, FF, D), 1.0, 6.0, ((1, 32),), jnp.float32)
    expert_moment = gaussian(splits[3], (MATS, FF, D), 1.0, 6.0, ((1, 32),), jnp.float32)
    table_master = gaussian(splits[4], (VOCAB, D), 1.0, 6.0, ((0, 32),), jnp.float32)
    table_moment = gaussian(splits[5], (VOCAB, D), 1.0, 6.0, ((0, 32),), jnp.float32)
    return dict(expert_change=expert_change, table_change=table_change, expert_master=expert_master, expert_moment=expert_moment, table_master=table_master, table_moment=table_moment)


momentum_coef = 0.9
outer_rate = 0.7


def reference(expert_change, table_change, expert_master, expert_moment, table_master, table_moment):
    expert_mean = jnp.transpose(jnp.sum(expert_change, axis=0), (0, 2, 1)) / N_REP
    table_mean = jnp.transpose(jnp.sum(table_change, axis=0)) / N_REP
    expert_velocity = momentum_coef * expert_moment + expert_mean
    expert_weights = expert_master - outer_rate * (expert_mean + momentum_coef * expert_velocity)
    expert_copies = jnp.transpose(expert_weights, (0, 2, 1)).astype(jnp.bfloat16)
    table_velocity = momentum_coef * table_moment + table_mean
    table_weights = table_master - outer_rate * (table_mean + momentum_coef * table_velocity)
    table_copies = jnp.transpose(table_weights).astype(jnp.bfloat16)
    return (expert_weights, expert_velocity, expert_copies, table_weights, table_velocity, table_copies)
```

```python
import jax
import jax.numpy as jnp
from jax import lax
from jax.sharding import PartitionSpec as P

momentum_coef = 0.9
outer_rate = 0.7


def update(master, moment, mean):
    velocity = momentum_coef * moment + mean
    weights = master - outer_rate * (mean + momentum_coef * velocity)
    return weights, velocity


def local(expert_change, table_change, expert_master, expert_moment, table_master, table_moment):
    groups = lax.axis_size("rep")
    tensor = lax.axis_size("tp")
    shards = lax.axis_size("shard")
    t = lax.axis_index("tp")
    mats, width, half = expert_change.shape[1:]
    rows = expert_master.shape[1]
    vrows = table_master.shape[0]
    per_half = shards // tensor

    summed = lax.psum((expert_change[0], table_change[0]), "rep")
    ge = lax.all_gather(summed[0], "tp", axis=0)
    gt = lax.all_gather(summed[1], "tp", axis=0)

    se = ge.reshape(tensor, mats, width, per_half, rows)
    se = jnp.transpose(se, (0, 3, 1, 2, 4)).reshape(shards, mats, width, rows)
    st = gt.reshape(tensor, width, per_half, vrows)
    st = jnp.transpose(st, (0, 2, 1, 3)).reshape(shards, width, vrows)

    re = lax.all_to_all(se, "shard", 0, 0, tiled=True)
    rt = lax.all_to_all(st, "shard", 0, 0, tiled=True)

    expert_sum = jnp.transpose(re, (1, 3, 0, 2)).reshape(mats, rows, shards * width)
    table_sum = jnp.transpose(rt.reshape(shards * width, vrows))
    expert_weights, expert_velocity = update(expert_master, expert_moment, expert_sum / groups)
    table_weights, table_velocity = update(table_master, table_moment, table_sum / groups)

    le = expert_weights.astype(jnp.bfloat16).reshape(mats, rows, shards, width)
    le = jnp.transpose(le, (2, 0, 3, 1))
    lt = table_weights.astype(jnp.bfloat16).reshape(vrows, shards, width)
    lt = jnp.transpose(lt, (1, 2, 0))
    be = lax.all_to_all(le, "shard", 0, 0, tiled=True)
    bt = lax.all_to_all(lt, "shard", 0, 0, tiled=True)
    be = lax.dynamic_slice_in_dim(be, t * per_half, per_half, 0)
    bt = lax.dynamic_slice_in_dim(bt, t * per_half, per_half, 0)
    expert_copies = jnp.transpose(be, (1, 2, 0, 3)).reshape(mats, width, per_half * rows)
    table_copies = jnp.transpose(bt, (1, 0, 2)).reshape(width, per_half * vrows)
    return (
        expert_weights,
        expert_velocity,
        expert_copies,
        table_weights,
        table_velocity,
        table_copies,
    )


def solution(mesh):
    in_specs = (
        P("rep", None, "shard", "tp"),
        P("rep", "shard", "tp"),
        P(None, "shard", None),
        P(None, "shard", None),
        P("shard", None),
        P("shard", None),
    )
    out_specs = (
        P(None, "shard", None),
        P(None, "shard", None),
        P(None, "shard", "tp"),
        P("shard", None),
        P("shard", None),
        P("shard", "tp"),
    )
    return jax.shard_map(local, mesh=mesh, in_specs=in_specs, out_specs=out_specs, check_vma=False)
```

```python
import jax
import jax.numpy as jnp
from jax import lax
from jax.sharding import PartitionSpec as P

momentum_coef = 0.9
outer_rate = 0.7


def update(master, moment, mean):
    velocity = momentum_coef * moment + mean
    weights = master - outer_rate * (mean + momentum_coef * velocity)
    return weights, velocity


def local(expert_change, table_change, expert_master, expert_moment, table_master, table_moment):
    groups = lax.axis_size("rep")
    tensor = lax.axis_size("tp")
    shards = lax.axis_size("shard")
    t = lax.axis_index("tp")
    mats, width, half = expert_change.shape[1:]
    rows = expert_master.shape[1]
    vrows = table_master.shape[0]
    per_half = shards // tensor

    ex = expert_change[0]
    tx = table_change[0]
    flat = jnp.concatenate([ex.reshape(-1), tx.reshape(-1)])
    quarters = lax.all_to_all(flat.reshape(groups, -1), "rep", 0, 0, tiled=True)
    part = jnp.sum(quarters, axis=0)
    whole = lax.all_to_all(
        jnp.broadcast_to(part[None], (groups, part.size)), "rep", 0, 0, tiled=True
    ).reshape(-1)
    both = lax.all_to_all(
        jnp.broadcast_to(whole[None], (tensor, whole.size)), "tp", 0, 0, tiled=True
    )
    ge = both[:, : ex.size].reshape((tensor,) + ex.shape)
    gt = both[:, ex.size :].reshape((tensor,) + tx.shape)

    se = ge.reshape(tensor, mats, width, per_half, rows)
    se = jnp.transpose(se, (0, 3, 1, 2, 4)).reshape(shards, mats, width, rows)
    st = gt.reshape(tensor, width, per_half, vrows)
    st = jnp.transpose(st, (0, 2, 1, 3)).reshape(shards, width, vrows)

    re = lax.all_to_all(se, "shard", 0, 0, tiled=True)
    rt = lax.all_to_all(st, "shard", 0, 0, tiled=True)

    expert_sum = jnp.transpose(re, (1, 3, 0, 2)).reshape(mats, rows, shards * width)
    table_sum = jnp.transpose(rt.reshape(shards * width, vrows))
    expert_weights, expert_velocity = update(expert_master, expert_moment, expert_sum / groups)
    table_weights, table_velocity = update(table_master, table_moment, table_sum / groups)

    le = expert_weights.astype(jnp.bfloat16).reshape(mats, rows, shards, width)
    le = jnp.transpose(le, (2, 0, 3, 1))
    lt = table_weights.astype(jnp.bfloat16).reshape(vrows, shards, width)
    lt = jnp.transpose(lt, (1, 2, 0))
    be = lax.all_to_all(le, "shard", 0, 0, tiled=True)
    bt = lax.all_to_all(lt, "shard", 0, 0, tiled=True)
    be = lax.dynamic_slice_in_dim(be, t * per_half, per_half, 0)
    bt = lax.dynamic_slice_in_dim(bt, t * per_half, per_half, 0)
    expert_copies = jnp.transpose(be, (1, 2, 0, 3)).reshape(mats, width, per_half * rows)
    table_copies = jnp.transpose(bt, (1, 0, 2)).reshape(width, per_half * vrows)
    return (
        expert_weights,
        expert_velocity,
        expert_copies,
        table_weights,
        table_velocity,
        table_copies,
    )


def solution(mesh):
    in_specs = (
        P("rep", None, "shard", "tp"),
        P("rep", "shard", "tp"),
        P(None, "shard", None),
        P(None, "shard", None),
        P("shard", None),
        P("shard", None),
    )
    out_specs = (
        P(None, "shard", None),
        P(None, "shard", None),
        P(None, "shard", "tp"),
        P("shard", None),
        P("shard", None),
        P("shard", "tp"),
    )
    return jax.shard_map(local, mesh=mesh, in_specs=in_specs, out_specs=out_specs, check_vma=False)
```

```python
import jax
import jax.numpy as jnp
from jax import lax
from jax.sharding import PartitionSpec as P

momentum_coef = 0.9
outer_rate = 0.7


def update(master, moment, mean):
    velocity = momentum_coef * moment + mean
    weights = master - outer_rate * (mean + momentum_coef * velocity)
    return weights, velocity


def pairs(n, flip):
    return [(i, i ^ flip) for i in range(n)]


def rep_scatter(x):
    r = lax.axis_index("rep")
    n = lax.axis_size("rep")
    core, x_lo = r % 2, r // 2
    x4 = x.reshape(2, 2, -1)
    mine = lax.dynamic_index_in_dim(x4, core, 1, keepdims=False)
    other = lax.dynamic_index_in_dim(x4, 1 - core, 1, keepdims=False)
    a = mine + lax.ppermute(other, "rep", pairs(n, 1))
    keep = lax.dynamic_index_in_dim(a, x_lo, 0, keepdims=False)
    send = lax.dynamic_index_in_dim(a, 1 - x_lo, 0, keepdims=False)
    return keep + lax.ppermute(send, "rep", pairs(n, 2))


def rep_gather(x):
    r = lax.axis_index("rep")
    n = lax.axis_size("rep")
    core, x_lo = r % 2, r // 2
    cross = lax.ppermute(x, "rep", pairs(n, 2))
    pair = jnp.where(x_lo == 0, jnp.stack([x, cross]), jnp.stack([cross, x]))
    sib = lax.ppermute(pair, "rep", pairs(n, 1))
    full = jnp.where(core == 0, jnp.stack([pair, sib], 1), jnp.stack([sib, pair], 1))
    return full.reshape((n,) + x.shape)


def local(expert_change, table_change, expert_master, expert_moment, table_master, table_moment):
    groups = lax.axis_size("rep")
    tensor = lax.axis_size("tp")
    shards = lax.axis_size("shard")
    t = lax.axis_index("tp")
    mats, width, half = expert_change.shape[1:]
    rows = expert_master.shape[1]
    vrows = table_master.shape[0]
    per_half = shards // tensor
    sub = vrows // groups
    esize = width * half

    ex = expert_change[0].reshape(mats, esize)
    tx = table_change[0].reshape(width, per_half, groups, sub)
    tx = jnp.transpose(tx, (2, 0, 1, 3)).reshape(groups, -1)
    q = rep_scatter(jnp.concatenate([ex, tx], axis=1))

    other = lax.ppermute(q, "tp", pairs(tensor, 1))
    halves = jnp.where(t == 0, jnp.stack([q, other]), jnp.stack([other, q]))
    he = halves[:, :esize].reshape(tensor, width, per_half, rows)
    he = jnp.transpose(he, (0, 2, 1, 3)).reshape(shards, width * rows)
    ht = halves[:, esize:].reshape(tensor, width, per_half, sub)
    ht = jnp.transpose(ht, (0, 2, 1, 3)).reshape(shards, width * sub)
    got = lax.all_to_all(jnp.concatenate([he, ht], 1), "shard", 0, 0, tiled=True)

    every = rep_gather(got)
    ee = every[:, :, : width * rows].reshape(groups, shards, width, rows)
    expert_sum = jnp.transpose(ee, (0, 3, 1, 2)).reshape(mats, rows, shards * width)
    et = every[:, :, width * rows :].reshape(groups, shards, width, sub)
    table_sum = jnp.transpose(et, (0, 3, 1, 2)).reshape(vrows, shards * width)

    expert_weights, expert_velocity = update(expert_master, expert_moment, expert_sum / groups)
    table_weights, table_velocity = update(table_master, table_moment, table_sum / groups)

    r = lax.axis_index("rep")
    le = lax.dynamic_index_in_dim(expert_weights, r, 0, keepdims=False)
    le = le.astype(jnp.bfloat16).reshape(rows, shards, width)
    le = jnp.transpose(le, (1, 2, 0)).reshape(shards, width * rows)
    lt = lax.dynamic_slice_in_dim(table_weights, r * sub, sub, 0)
    lt = lt.astype(jnp.bfloat16).reshape(sub, shards, width)
    lt = jnp.transpose(lt, (1, 2, 0)).reshape(shards, width * sub)
    back = lax.all_to_all(jnp.concatenate([le, lt], 1), "shard", 0, 0, tiled=True)
    back = lax.dynamic_slice_in_dim(back, t * per_half, per_half, 0)
    allq = rep_gather(back)
    ce = allq[:, :, : width * rows].reshape(groups, per_half, width, rows)
    expert_copies = jnp.transpose(ce, (0, 2, 1, 3)).reshape(mats, width, per_half * rows)
    ct = allq[:, :, width * rows :].reshape(groups, per_half, width, sub)
    table_copies = jnp.transpose(ct, (2, 1, 0, 3)).reshape(width, per_half * vrows)
    return (
        expert_weights,
        expert_velocity,
        expert_copies,
        table_weights,
        table_velocity,
        table_copies,
    )


def solution(mesh):
    in_specs = (
        P("rep", None, "shard", "tp"),
        P("rep", "shard", "tp"),
        P(None, "shard", None),
        P(None, "shard", None),
        P("shard", None),
        P("shard", None),
    )
    out_specs = (
        P(None, "shard", None),
        P(None, "shard", None),
        P(None, "shard", "tp"),
        P("shard", None),
        P("shard", None),
        P("shard", "tp"),
    )
    return jax.shard_map(local, mesh=mesh, in_specs=in_specs, out_specs=out_specs, check_vma=False)
```

```python
import jax
import jax.numpy as jnp
from jax import lax
from jax.sharding import PartitionSpec as P
from jax.experimental import pallas as pl
from jax.experimental.pallas import tpu as pltpu

momentum_coef = 0.9
outer_rate = 0.7


def update(master, moment, mean):
    velocity = momentum_coef * moment + mean
    weights = master - outer_rate * (mean + momentum_coef * velocity)
    return weights, velocity


def pairs(n, flip):
    return [(i, i ^ flip) for i in range(n)]


def rep_scatter(x):
    r = lax.axis_index("rep")
    n = lax.axis_size("rep")
    core, x_lo = r % 2, r // 2
    x4 = x.reshape(2, 2, -1)
    mine = lax.dynamic_index_in_dim(x4, core, 1, keepdims=False)
    other = lax.dynamic_index_in_dim(x4, 1 - core, 1, keepdims=False)
    a = mine + lax.ppermute(other, "rep", pairs(n, 1))
    keep = lax.dynamic_index_in_dim(a, x_lo, 0, keepdims=False)
    send = lax.dynamic_index_in_dim(a, 1 - x_lo, 0, keepdims=False)
    return keep + lax.ppermute(send, "rep", pairs(n, 2))


def rep_gather(x):
    r = lax.axis_index("rep")
    n = lax.axis_size("rep")
    core, x_lo = r % 2, r // 2
    cross = lax.ppermute(x, "rep", pairs(n, 2))
    pair = jax.tree.map(
        lambda a, b: jnp.where(x_lo == 0, jnp.stack([a, b]), jnp.stack([b, a])), x, cross
    )
    sib = lax.ppermute(pair, "rep", pairs(n, 1))
    full = jax.tree.map(
        lambda a, b: jnp.where(core == 0, jnp.stack([a, b], 1), jnp.stack([b, a], 1)), pair, sib
    )
    return jax.tree.map(lambda a, f: f.reshape((n,) + a.shape), x, full)


def update_kernel(scale, mean_ref, master_ref, moment_ref, w_ref, v_ref, low_ref):
    x = mean_ref[0]
    x = x.reshape(x.shape[0] * x.shape[1], x.shape[2])
    mean = x.T * scale
    weights, velocity = update(master_ref[...], moment_ref[...], mean.reshape(master_ref.shape))
    w_ref[...] = weights
    v_ref[...] = velocity
    low_ref[0] = weights.reshape(mean.shape).T.astype(low_ref.dtype)


def fused_update(got, master, moment, scale):
    quarters, srcs, wdt, cols = got.shape
    lead = master.shape[:-2]
    blk = (1,) * len(lead) + master.shape[-2:] if lead else (cols,) + master.shape[-1:]
    if lead:
        idx = lambda q: (q, 0, 0)
    else:
        idx = lambda q: (q, 0)
    big = pl.BlockSpec(blk, idx)
    return pl.pallas_call(
        lambda *refs: update_kernel(scale, *refs),
        grid=(quarters,),
        in_specs=[pl.BlockSpec((1, srcs, wdt, cols), lambda q: (q, 0, 0, 0)), big, big],
        out_specs=[big, big, pl.BlockSpec((1, srcs * wdt, cols), lambda q: (q, 0, 0))],
        out_shape=[
            jax.ShapeDtypeStruct(master.shape, master.dtype),
            jax.ShapeDtypeStruct(master.shape, master.dtype),
            jax.ShapeDtypeStruct((quarters, srcs * wdt, cols), jnp.bfloat16),
        ],
    )(got, master, moment)


def local(expert_change, table_change, expert_master, expert_moment, table_master, table_moment):
    groups = lax.axis_size("rep")
    tensor = lax.axis_size("tp")
    shards = lax.axis_size("shard")
    t = lax.axis_index("tp")
    mats, width, half = expert_change.shape[1:]
    rows = expert_master.shape[1]
    vrows = table_master.shape[0]
    per_half = shards // tensor
    sub = vrows // groups
    esize = width * half

    ex = expert_change[0].reshape(mats, esize)
    tx = table_change[0].reshape(width, per_half, groups, sub)
    tx = jnp.transpose(tx, (2, 0, 1, 3)).reshape(groups, -1)
    q = rep_scatter(jnp.concatenate([ex, tx], axis=1))

    other = lax.ppermute(q, "tp", pairs(tensor, 1))
    halves = jnp.where(t == 0, jnp.stack([q, other]), jnp.stack([other, q]))
    he = halves[:, :esize].reshape(tensor, width, per_half, rows)
    he = jnp.transpose(he, (0, 2, 1, 3)).reshape(shards, width * rows)
    ht = halves[:, esize:].reshape(tensor, width, per_half, sub)
    ht = jnp.transpose(ht, (0, 2, 1, 3)).reshape(shards, width * sub)
    got = lax.all_to_all(jnp.concatenate([he, ht], 1), "shard", 0, 0, tiled=True)

    ge = got[:, : width * rows].reshape(shards, width, rows)
    gt = got[:, width * rows :].reshape(shards, width, sub)
    every_e, every_t = rep_gather((ge, gt))

    expert_weights, expert_velocity, low_e = fused_update(
        every_e, expert_master, expert_moment, 1.0 / groups
    )
    table_weights, table_velocity, low_t = fused_update(
        every_t, table_master, table_moment, 1.0 / groups
    )

    r = lax.axis_index("rep")
    le = lax.dynamic_index_in_dim(low_e, r, 0, keepdims=False).reshape(shards, width * rows)
    lt = lax.dynamic_index_in_dim(low_t, r, 0, keepdims=False).reshape(shards, width * sub)
    back = lax.all_to_all(jnp.concatenate([le, lt], 1), "shard", 0, 0, tiled=True)
    back = lax.dynamic_slice_in_dim(back, t * per_half, per_half, 0)
    allq = rep_gather(back)
    ce = allq[:, :, : width * rows].reshape(groups, per_half, width, rows)
    expert_copies = jnp.transpose(ce, (0, 2, 1, 3)).reshape(mats, width, per_half * rows)
    ct = allq[:, :, width * rows :].reshape(groups, per_half, width, sub)
    table_copies = jnp.transpose(ct, (2, 1, 0, 3)).reshape(width, per_half * vrows)
    return (
        expert_weights,
        expert_velocity,
        expert_copies,
        table_weights,
        table_velocity,
        table_copies,
    )


def solution(mesh):
    in_specs = (
        P("rep", None, "shard", "tp"),
        P("rep", "shard", "tp"),
        P(None, "shard", None),
        P(None, "shard", None),
        P("shard", None),
        P("shard", None),
    )
    out_specs = (
        P(None, "shard", None),
        P(None, "shard", None),
        P(None, "shard", "tp"),
        P("shard", None),
        P("shard", None),
        P("shard", "tp"),
    )
    return jax.shard_map(local, mesh=mesh, in_specs=in_specs, out_specs=out_specs, check_vma=False)
```

```python
import jax
import jax.numpy as jnp
from jax import lax
from jax.sharding import PartitionSpec as P
from jax.experimental import pallas as pl
from jax.experimental.pallas import tpu as pltpu

momentum_coef = 0.9
outer_rate = 0.7


def update(master, moment, mean):
    velocity = momentum_coef * moment + mean
    weights = master - outer_rate * (mean + momentum_coef * velocity)
    return weights, velocity


def pairs(n, flip):
    return [(i, i ^ flip) for i in range(n)]


def rep_scatter(x):
    r = lax.axis_index("rep")
    n = lax.axis_size("rep")
    core, x_lo = r % 2, r // 2
    x4 = x.reshape(2, 2, -1)
    mine = lax.dynamic_index_in_dim(x4, core, 1, keepdims=False)
    other = lax.dynamic_index_in_dim(x4, 1 - core, 1, keepdims=False)
    a = mine + lax.ppermute(other, "rep", pairs(n, 1))
    keep = lax.dynamic_index_in_dim(a, x_lo, 0, keepdims=False)
    send = lax.dynamic_index_in_dim(a, 1 - x_lo, 0, keepdims=False)
    return keep + lax.ppermute(send, "rep", pairs(n, 2))


def rep_gather(x):
    r = lax.axis_index("rep")
    n = lax.axis_size("rep")
    core, x_lo = r % 2, r // 2
    cross = lax.ppermute(x, "rep", pairs(n, 2))
    pair = jax.tree.map(
        lambda a, b: jnp.where(x_lo == 0, jnp.stack([a, b]), jnp.stack([b, a])), x, cross
    )
    sib = lax.ppermute(pair, "rep", pairs(n, 1))
    full = jax.tree.map(
        lambda a, b: jnp.where(core == 0, jnp.stack([a, b], 1), jnp.stack([b, a], 1)), pair, sib
    )
    return jax.tree.map(lambda a, f: f.reshape((n,) + a.shape), x, full)


def update_kernel(scale, mean_ref, master_ref, moment_ref, w_ref, v_ref, low_ref):
    x = mean_ref[0]
    x = x.reshape(x.shape[0] * x.shape[1], x.shape[2])
    mean = x.T * scale
    weights, velocity = update(master_ref[...], moment_ref[...], mean.reshape(master_ref.shape))
    w_ref[...] = weights
    v_ref[...] = velocity
    low_ref[0] = weights.reshape(mean.shape).T.astype(low_ref.dtype)


def fused_update(got, master, moment, scale):
    quarters, srcs, wdt, cols = got.shape
    lead = master.shape[:-2]
    blk = (1,) * len(lead) + master.shape[-2:] if lead else (cols,) + master.shape[-1:]
    if lead:
        idx = lambda q: (q, 0, 0)
    else:
        idx = lambda q: (q, 0)
    big = pl.BlockSpec(blk, idx)
    return pl.pallas_call(
        lambda *refs: update_kernel(scale, *refs),
        grid=(quarters,),
        in_specs=[pl.BlockSpec((1, srcs, wdt, cols), lambda q: (q, 0, 0, 0)), big, big],
        out_specs=[big, big, pl.BlockSpec((1, srcs * wdt, cols), lambda q: (q, 0, 0))],
        out_shape=[
            jax.ShapeDtypeStruct(master.shape, master.dtype),
            jax.ShapeDtypeStruct(master.shape, master.dtype),
            jax.ShapeDtypeStruct((quarters, srcs * wdt, cols), jnp.bfloat16),
        ],
    )(got, master, moment)


def shard_all_to_all(x):
    n = x.shape[0]

    def copy(x_ref, y_ref, send, recv, src, dst, peer):
        return pltpu.make_async_remote_copy(
            src_ref=x_ref.at[src],
            dst_ref=y_ref.at[dst],
            send_sem=send.at[src],
            recv_sem=recv.at[dst],
            device_id={"shard": peer},
            device_id_type=pl.DeviceIdType.MESH,
        )

    def kernel(x_ref, y_ref, send, recv, local_sem):
        me = lax.axis_index("shard")
        local = pltpu.make_async_copy(x_ref.at[me], y_ref.at[me], local_sem)
        local.start()

        def start(i, c):
            k = lax.rem(me + i, n)
            copy(x_ref, y_ref, send, recv, k, me, k).start()
            return c

        lax.fori_loop(1, n, start, 0)

        def wait(i, c):
            k = lax.rem(me + i, n)
            src = lax.rem(me + n - i, n)
            copy(x_ref, y_ref, send, recv, k, me, k).wait_send()
            copy(x_ref, y_ref, send, recv, src, src, src).wait_recv()
            return c

        lax.fori_loop(1, n, wait, 0)
        local.wait()

    return pl.pallas_call(
        kernel,
        out_shape=jax.ShapeDtypeStruct(x.shape, x.dtype),
        in_specs=[pl.BlockSpec(memory_space=pl.ANY)],
        out_specs=pl.BlockSpec(memory_space=pl.ANY),
        scratch_shapes=[
            pltpu.SemaphoreType.DMA((n,)),
            pltpu.SemaphoreType.DMA((n,)),
            pltpu.SemaphoreType.DMA,
        ],
        compiler_params=pltpu.CompilerParams(has_side_effects=True),
    )(x)


def local(expert_change, table_change, expert_master, expert_moment, table_master, table_moment):
    groups = lax.axis_size("rep")
    tensor = lax.axis_size("tp")
    shards = lax.axis_size("shard")
    t = lax.axis_index("tp")
    mats, width, half = expert_change.shape[1:]
    rows = expert_master.shape[1]
    vrows = table_master.shape[0]
    per_half = shards // tensor
    sub = vrows // groups
    esize = width * half

    ex = expert_change[0].reshape(mats, esize)
    tx = table_change[0].reshape(width, per_half, groups, sub)
    tx = jnp.transpose(tx, (2, 0, 1, 3)).reshape(groups, -1)
    q = rep_scatter(jnp.concatenate([ex, tx], axis=1))

    other = lax.ppermute(q, "tp", pairs(tensor, 1))
    halves = jnp.where(t == 0, jnp.stack([q, other]), jnp.stack([other, q]))
    he = halves[:, :esize].reshape(tensor, width, per_half, rows)
    he = jnp.transpose(he, (0, 2, 1, 3)).reshape(shards, width * rows)
    ht = halves[:, esize:].reshape(tensor, width, per_half, sub)
    ht = jnp.transpose(ht, (0, 2, 1, 3)).reshape(shards, width * sub)
    got = shard_all_to_all(jnp.concatenate([he, ht], 1)[:, None])[:, 0]

    ge = got[:, : width * rows].reshape(shards, width, rows)
    gt = got[:, width * rows :].reshape(shards, width, sub)
    every_e, every_t = rep_gather((ge, gt))

    expert_weights, expert_velocity, low_e = fused_update(
        every_e, expert_master, expert_moment, 1.0 / groups
    )
    table_weights, table_velocity, low_t = fused_update(
        every_t, table_master, table_moment, 1.0 / groups
    )

    r = lax.axis_index("rep")
    le = lax.dynamic_index_in_dim(low_e, r, 0, keepdims=False).reshape(shards, width * rows)
    lt = lax.dynamic_index_in_dim(low_t, r, 0, keepdims=False).reshape(shards, width * sub)
    back = jnp.concatenate([le, lt], 1)
    back = shard_all_to_all(back.reshape(shards, 2, -1)).reshape(shards, -1)
    back = lax.dynamic_slice_in_dim(back, t * per_half, per_half, 0)
    allq = rep_gather(back)
    ce = allq[:, :, : width * rows].reshape(groups, per_half, width, rows)
    expert_copies = jnp.transpose(ce, (0, 2, 1, 3)).reshape(mats, width, per_half * rows)
    ct = allq[:, :, width * rows :].reshape(groups, per_half, width, sub)
    table_copies = jnp.transpose(ct, (2, 1, 0, 3)).reshape(width, per_half * vrows)
    return (
        expert_weights,
        expert_velocity,
        expert_copies,
        table_weights,
        table_velocity,
        table_copies,
    )


def solution(mesh):
    in_specs = (
        P("rep", None, "shard", "tp"),
        P("rep", "shard", "tp"),
        P(None, "shard", None),
        P(None, "shard", None),
        P("shard", None),
        P("shard", None),
    )
    out_specs = (
        P(None, "shard", None),
        P(None, "shard", None),
        P(None, "shard", "tp"),
        P("shard", None),
        P("shard", None),
        P("shard", "tp"),
    )
    return jax.shard_map(local, mesh=mesh, in_specs=in_specs, out_specs=out_specs, check_vma=False)
```

```python
import jax
import jax.numpy as jnp
from jax import lax
from jax.sharding import PartitionSpec as P
from jax.experimental import pallas as pl
from jax.experimental.pallas import tpu as pltpu

momentum_coef = 0.9
outer_rate = 0.7


def update(master, moment, mean):
    velocity = momentum_coef * moment + mean
    weights = master - outer_rate * (mean + momentum_coef * velocity)
    return weights, velocity


def pairs(n, flip):
    return [(i, i ^ flip) for i in range(n)]


def rep_scatter(x):
    r = lax.axis_index("rep")
    n = lax.axis_size("rep")
    core, x_lo = r % 2, r // 2
    x4 = x.reshape(2, 2, -1)
    mine = lax.dynamic_index_in_dim(x4, core, 1, keepdims=False)
    other = lax.dynamic_index_in_dim(x4, 1 - core, 1, keepdims=False)
    a = mine + lax.ppermute(other, "rep", pairs(n, 1))
    keep = lax.dynamic_index_in_dim(a, x_lo, 0, keepdims=False)
    send = lax.dynamic_index_in_dim(a, 1 - x_lo, 0, keepdims=False)
    return keep + lax.ppermute(send, "rep", pairs(n, 2))


def rep_gather(x):
    r = lax.axis_index("rep")
    n = lax.axis_size("rep")
    core, x_lo = r % 2, r // 2
    cross = lax.ppermute(x, "rep", pairs(n, 2))
    pair = jax.tree.map(
        lambda a, b: jnp.where(x_lo == 0, jnp.stack([a, b]), jnp.stack([b, a])), x, cross
    )
    sib = lax.ppermute(pair, "rep", pairs(n, 1))
    full = jax.tree.map(
        lambda a, b: jnp.where(core == 0, jnp.stack([a, b], 1), jnp.stack([b, a], 1)), pair, sib
    )
    return jax.tree.map(lambda a, f: f.reshape((n,) + a.shape), x, full)


def update_kernel(scale, mean_ref, master_ref, moment_ref, w_ref, v_ref, low_ref):
    x = mean_ref[0]
    x = x.reshape(x.shape[0] * x.shape[1], x.shape[2])
    mean = x.T * scale
    weights, velocity = update(master_ref[...], moment_ref[...], mean.reshape(master_ref.shape))
    w_ref[...] = weights
    v_ref[...] = velocity
    low_ref[0] = weights.reshape(mean.shape).T.astype(low_ref.dtype)


def fused_update(got, master, moment, scale):
    quarters, srcs, wdt, cols = got.shape
    lead = master.shape[:-2]
    blk = (1,) * len(lead) + master.shape[-2:] if lead else (cols,) + master.shape[-1:]
    if lead:
        idx = lambda q: (q, 0, 0)
    else:
        idx = lambda q: (q, 0)
    big = pl.BlockSpec(blk, idx)
    return pl.pallas_call(
        lambda *refs: update_kernel(scale, *refs),
        grid=(quarters,),
        in_specs=[pl.BlockSpec((1, srcs, wdt, cols), lambda q: (q, 0, 0, 0)), big, big],
        out_specs=[big, big, pl.BlockSpec((1, srcs * wdt, cols), lambda q: (q, 0, 0))],
        out_shape=[
            jax.ShapeDtypeStruct(master.shape, master.dtype),
            jax.ShapeDtypeStruct(master.shape, master.dtype),
            jax.ShapeDtypeStruct((quarters, srcs * wdt, cols), jnp.bfloat16),
        ],
    )(got, master, moment)


def local(expert_change, table_change, expert_master, expert_moment, table_master, table_moment):
    groups = lax.axis_size("rep")
    tensor = lax.axis_size("tp")
    shards = lax.axis_size("shard")
    t = lax.axis_index("tp")
    mats, width, half = expert_change.shape[1:]
    rows = expert_master.shape[1]
    vrows = table_master.shape[0]
    per_half = shards // tensor
    sub = vrows // groups
    esize = width * half

    r = lax.axis_index("rep")

    def forward(x, cols):
        q = rep_scatter(x)
        other = lax.ppermute(q, "tp", pairs(tensor, 1))
        h = jnp.where(t == 0, jnp.stack([q, other]), jnp.stack([other, q]))
        h = jnp.transpose(h.reshape(tensor, width, per_half, cols), (0, 2, 1, 3))
        got = lax.all_to_all(h.reshape(shards, width * cols), "shard", 0, 0, tiled=True)
        return rep_gather(got.reshape(shards, width, cols))

    def backward(low, cols):
        mine = lax.dynamic_index_in_dim(low, r, 0, keepdims=False).reshape(shards, width * cols)
        back = lax.all_to_all(mine, "shard", 0, 0, tiled=True)
        back = lax.dynamic_slice_in_dim(back, t * per_half, per_half, 0)
        return rep_gather(back.reshape(per_half, width, cols))

    ex = expert_change[0].reshape(mats, esize)
    tx = table_change[0].reshape(width, per_half, groups, sub)
    tx = jnp.transpose(tx, (2, 0, 1, 3)).reshape(groups, -1)
    every_e = forward(ex, rows)
    every_t = forward(tx, sub)

    expert_weights, expert_velocity, low_e = fused_update(
        every_e, expert_master, expert_moment, 1.0 / groups
    )
    table_weights, table_velocity, low_t = fused_update(
        every_t, table_master, table_moment, 1.0 / groups
    )

    ce = backward(low_e, rows)
    expert_copies = jnp.transpose(ce, (0, 2, 1, 3)).reshape(mats, width, per_half * rows)
    ct = backward(low_t, sub)
    table_copies = jnp.transpose(ct, (2, 1, 0, 3)).reshape(width, per_half * vrows)
    return (
        expert_weights,
        expert_velocity,
        expert_copies,
        table_weights,
        table_velocity,
        table_copies,
    )


def solution(mesh):
    in_specs = (
        P("rep", None, "shard", "tp"),
        P("rep", "shard", "tp"),
        P(None, "shard", None),
        P(None, "shard", None),
        P("shard", None),
        P("shard", None),
    )
    out_specs = (
        P(None, "shard", None),
        P(None, "shard", None),
        P(None, "shard", "tp"),
        P("shard", None),
        P("shard", None),
        P("shard", "tp"),
    )
    return jax.shard_map(local, mesh=mesh, in_specs=in_specs, out_specs=out_specs, check_vma=False)
```

```python
import jax
import jax.numpy as jnp
from jax import lax
from jax.sharding import PartitionSpec as P
from jax.experimental import pallas as pl
from jax.experimental.pallas import tpu as pltpu

momentum_coef = 0.9
outer_rate = 0.7


def update(master, moment, mean):
    velocity = momentum_coef * moment + mean
    weights = master - outer_rate * (mean + momentum_coef * velocity)
    return weights, velocity


def pairs(n, flip):
    return [(i, i ^ flip) for i in range(n)]


def scatter_both_halves(x):
    r = lax.axis_index("rep")
    n = lax.axis_size("rep")
    t = lax.axis_index("tp")
    tensor = lax.axis_size("tp")
    core, x_lo = r % 2, r // 2
    x4 = x.reshape(2, 2, -1)
    mine = lax.dynamic_index_in_dim(x4, core, 1, keepdims=False)
    other = lax.dynamic_index_in_dim(x4, 1 - core, 1, keepdims=False)
    a = mine + lax.ppermute(other, "rep", pairs(n, 1))
    keep = lax.dynamic_index_in_dim(a, x_lo, 0, keepdims=False)
    send = lax.dynamic_index_in_dim(a, 1 - x_lo, 0, keepdims=False)
    diagonal = [
        (i * tensor + j, (i ^ 2) * tensor + (j ^ 1)) for i in range(n) for j in range(tensor)
    ]
    from_cross = lax.ppermute(send, "rep", pairs(n, 2))
    from_partner = lax.ppermute(keep, "tp", pairs(tensor, 1))
    from_diagonal = lax.ppermute(send, ("rep", "tp"), diagonal)
    own = keep + from_cross
    far = from_partner + from_diagonal
    return jnp.where(t == 0, jnp.stack([own, far]), jnp.stack([far, own]))


def rep_gather(x):
    r = lax.axis_index("rep")
    n = lax.axis_size("rep")
    core, x_lo = r % 2, r // 2
    cross = lax.ppermute(x, "rep", pairs(n, 2))
    pair = jax.tree.map(
        lambda a, b: jnp.where(x_lo == 0, jnp.stack([a, b]), jnp.stack([b, a])), x, cross
    )
    sib = lax.ppermute(pair, "rep", pairs(n, 1))
    full = jax.tree.map(
        lambda a, b: jnp.where(core == 0, jnp.stack([a, b], 1), jnp.stack([b, a], 1)), pair, sib
    )
    return jax.tree.map(lambda a, f: f.reshape((n,) + a.shape), x, full)


def update_kernel(scale, mean_ref, master_ref, moment_ref, w_ref, v_ref, low_ref):
    x = mean_ref[0]
    x = x.reshape(x.shape[0] * x.shape[1], x.shape[2])
    mean = x.T * scale
    weights, velocity = update(master_ref[...], moment_ref[...], mean.reshape(master_ref.shape))
    w_ref[...] = weights
    v_ref[...] = velocity
    low_ref[0] = weights.reshape(mean.shape).T.astype(low_ref.dtype)


def fused_update(got, master, moment, scale):
    quarters, srcs, wdt, cols = got.shape
    lead = master.shape[:-2]
    blk = (1,) * len(lead) + master.shape[-2:] if lead else (cols,) + master.shape[-1:]
    if lead:
        idx = lambda q: (q, 0, 0)
    else:
        idx = lambda q: (q, 0)
    big = pl.BlockSpec(blk, idx)
    return pl.pallas_call(
        lambda *refs: update_kernel(scale, *refs),
        grid=(quarters,),
        in_specs=[pl.BlockSpec((1, srcs, wdt, cols), lambda q: (q, 0, 0, 0)), big, big],
        out_specs=[big, big, pl.BlockSpec((1, srcs * wdt, cols), lambda q: (q, 0, 0))],
        out_shape=[
            jax.ShapeDtypeStruct(master.shape, master.dtype),
            jax.ShapeDtypeStruct(master.shape, master.dtype),
            jax.ShapeDtypeStruct((quarters, srcs * wdt, cols), jnp.bfloat16),
        ],
    )(got, master, moment)


def local(expert_change, table_change, expert_master, expert_moment, table_master, table_moment):
    groups = lax.axis_size("rep")
    tensor = lax.axis_size("tp")
    shards = lax.axis_size("shard")
    t = lax.axis_index("tp")
    mats, width, half = expert_change.shape[1:]
    rows = expert_master.shape[1]
    vrows = table_master.shape[0]
    per_half = shards // tensor
    sub = vrows // groups
    esize = width * half

    ex = expert_change[0].reshape(mats, esize)
    tx = table_change[0].reshape(width, per_half, groups, sub)
    tx = jnp.transpose(tx, (2, 0, 1, 3)).reshape(groups, -1)
    halves = scatter_both_halves(jnp.concatenate([ex, tx], axis=1))
    he = halves[:, :esize].reshape(tensor, width, per_half, rows)
    he = jnp.transpose(he, (0, 2, 1, 3)).reshape(shards, width * rows)
    ht = halves[:, esize:].reshape(tensor, width, per_half, sub)
    ht = jnp.transpose(ht, (0, 2, 1, 3)).reshape(shards, width * sub)
    got = lax.all_to_all(jnp.concatenate([he, ht], 1), "shard", 0, 0, tiled=True)

    ge = got[:, : width * rows].reshape(shards, width, rows)
    gt = got[:, width * rows :].reshape(shards, width, sub)
    every_e, every_t = rep_gather((ge, gt))

    expert_weights, expert_velocity, low_e = fused_update(
        every_e, expert_master, expert_moment, 1.0 / groups
    )
    table_weights, table_velocity, low_t = fused_update(
        every_t, table_master, table_moment, 1.0 / groups
    )

    r = lax.axis_index("rep")
    le = lax.dynamic_index_in_dim(low_e, r, 0, keepdims=False).reshape(shards, width * rows)
    lt = lax.dynamic_index_in_dim(low_t, r, 0, keepdims=False).reshape(shards, width * sub)
    back = lax.all_to_all(jnp.concatenate([le, lt], 1), "shard", 0, 0, tiled=True)
    back = lax.dynamic_slice_in_dim(back, t * per_half, per_half, 0)
    allq = rep_gather(back)
    ce = allq[:, :, : width * rows].reshape(groups, per_half, width, rows)
    expert_copies = jnp.transpose(ce, (0, 2, 1, 3)).reshape(mats, width, per_half * rows)
    ct = allq[:, :, width * rows :].reshape(groups, per_half, width, sub)
    table_copies = jnp.transpose(ct, (2, 1, 0, 3)).reshape(width, per_half * vrows)
    return (
        expert_weights,
        expert_velocity,
        expert_copies,
        table_weights,
        table_velocity,
        table_copies,
    )


def solution(mesh):
    in_specs = (
        P("rep", None, "shard", "tp"),
        P("rep", "shard", "tp"),
        P(None, "shard", None),
        P(None, "shard", None),
        P("shard", None),
        P("shard", None),
    )
    out_specs = (
        P(None, "shard", None),
        P(None, "shard", None),
        P(None, "shard", "tp"),
        P("shard", None),
        P("shard", None),
        P("shard", "tp"),
    )
    return jax.shard_map(local, mesh=mesh, in_specs=in_specs, out_specs=out_specs, check_vma=False)
```

```python
import jax
import jax.numpy as jnp
from jax import lax
from jax.sharding import PartitionSpec as P
from jax.experimental import pallas as pl
from jax.experimental.pallas import tpu as pltpu

momentum_coef = 0.9
outer_rate = 0.7


def update(master, moment, mean):
    velocity = momentum_coef * moment + mean
    weights = master - outer_rate * (mean + momentum_coef * velocity)
    return weights, velocity


def pairs(n, flip):
    return [(i, i ^ flip) for i in range(n)]


def rep_scatter(x):
    r = lax.axis_index("rep")
    n = lax.axis_size("rep")
    core, x_lo = r % 2, r // 2
    x4 = x.reshape(2, 2, -1)
    mine = lax.dynamic_index_in_dim(x4, core, 1, keepdims=False)
    other = lax.dynamic_index_in_dim(x4, 1 - core, 1, keepdims=False)
    a = mine + lax.ppermute(other, "rep", pairs(n, 1))
    keep = lax.dynamic_index_in_dim(a, x_lo, 0, keepdims=False)
    send = lax.dynamic_index_in_dim(a, 1 - x_lo, 0, keepdims=False)
    return keep + lax.ppermute(send, "rep", pairs(n, 2))


def rep_gather(x):
    r = lax.axis_index("rep")
    n = lax.axis_size("rep")
    core, x_lo = r % 2, r // 2
    cross = lax.ppermute(x, "rep", pairs(n, 2))
    pair = jax.tree.map(
        lambda a, b: jnp.where(x_lo == 0, jnp.stack([a, b]), jnp.stack([b, a])), x, cross
    )
    sib = lax.ppermute(pair, "rep", pairs(n, 1))
    full = jax.tree.map(
        lambda a, b: jnp.where(core == 0, jnp.stack([a, b], 1), jnp.stack([b, a], 1)), pair, sib
    )
    return jax.tree.map(lambda a, f: f.reshape((n,) + a.shape), x, full)


def update_kernel(scale, mean_ref, master_ref, moment_ref, w_ref, v_ref):
    x = mean_ref[0]
    x = x.reshape(x.shape[0] * x.shape[1], x.shape[2])
    mean = x.T * scale
    weights, velocity = update(master_ref[...], moment_ref[...], mean.reshape(master_ref.shape))
    w_ref[...] = weights
    v_ref[...] = velocity


def fused_update(got, master, moment, scale):
    quarters, srcs, wdt, cols = got.shape
    lead = master.shape[:-2]
    blk = (1,) * len(lead) + master.shape[-2:] if lead else (cols,) + master.shape[-1:]
    if lead:
        idx = lambda q: (q, 0, 0)
    else:
        idx = lambda q: (q, 0)
    big = pl.BlockSpec(blk, idx)
    return pl.pallas_call(
        lambda *refs: update_kernel(scale, *refs),
        grid=(quarters,),
        in_specs=[pl.BlockSpec((1, srcs, wdt, cols), lambda q: (q, 0, 0, 0)), big, big],
        out_specs=[big, big],
        out_shape=[
            jax.ShapeDtypeStruct(master.shape, master.dtype),
            jax.ShapeDtypeStruct(master.shape, master.dtype),
        ],
    )(got, master, moment)


def local(expert_change, table_change, expert_master, expert_moment, table_master, table_moment):
    groups = lax.axis_size("rep")
    tensor = lax.axis_size("tp")
    shards = lax.axis_size("shard")
    t = lax.axis_index("tp")
    mats, width, half = expert_change.shape[1:]
    rows = expert_master.shape[1]
    vrows = table_master.shape[0]
    per_half = shards // tensor
    sub = vrows // groups
    esize = width * half

    ex = expert_change[0].reshape(mats, esize)
    tx = table_change[0].reshape(width, per_half, groups, sub)
    tx = jnp.transpose(tx, (2, 0, 1, 3)).reshape(groups, -1)
    q = rep_scatter(jnp.concatenate([ex, tx], axis=1))

    other = lax.ppermute(q, "tp", pairs(tensor, 1))
    halves = jnp.where(t == 0, jnp.stack([q, other]), jnp.stack([other, q]))
    he = halves[:, :esize].reshape(tensor, width, per_half, rows)
    he = jnp.transpose(he, (0, 2, 1, 3)).reshape(shards, width * rows)
    ht = halves[:, esize:].reshape(tensor, width, per_half, sub)
    ht = jnp.transpose(ht, (0, 2, 1, 3)).reshape(shards, width * sub)
    got = lax.all_to_all(jnp.concatenate([he, ht], 1), "shard", 0, 0, tiled=True)

    ge = got[:, : width * rows].reshape(shards, width, rows)
    gt = got[:, width * rows :].reshape(shards, width, sub)

    r = lax.axis_index("rep")
    own_e = jnp.transpose(ge.reshape(shards * width, rows)) / groups
    own_e, _ = update(
        lax.dynamic_index_in_dim(expert_master, r, 0, keepdims=False),
        lax.dynamic_index_in_dim(expert_moment, r, 0, keepdims=False),
        own_e,
    )
    le = jnp.transpose(own_e.astype(jnp.bfloat16).reshape(rows, shards, width), (1, 2, 0))
    own_t = jnp.transpose(gt.reshape(shards * width, sub)) / groups
    own_t, _ = update(
        lax.dynamic_slice_in_dim(table_master, r * sub, sub, 0),
        lax.dynamic_slice_in_dim(table_moment, r * sub, sub, 0),
        own_t,
    )
    lt = jnp.transpose(own_t.astype(jnp.bfloat16).reshape(sub, shards, width), (1, 2, 0))
    back = jnp.concatenate([le.reshape(shards, -1), lt.reshape(shards, -1)], 1)
    back = lax.all_to_all(back, "shard", 0, 0, tiled=True)

    every_e, every_t = rep_gather((ge, gt))
    expert_weights, expert_velocity = fused_update(
        every_e, expert_master, expert_moment, 1.0 / groups
    )
    table_weights, table_velocity = fused_update(
        every_t, table_master, table_moment, 1.0 / groups
    )

    back = lax.dynamic_slice_in_dim(back, t * per_half, per_half, 0)
    allq = rep_gather(back)
    ce = allq[:, :, : width * rows].reshape(groups, per_half, width, rows)
    expert_copies = jnp.transpose(ce, (0, 2, 1, 3)).reshape(mats, width, per_half * rows)
    ct = allq[:, :, width * rows :].reshape(groups, per_half, width, sub)
    table_copies = jnp.transpose(ct, (2, 1, 0, 3)).reshape(width, per_half * vrows)
    return (
        expert_weights,
        expert_velocity,
        expert_copies,
        table_weights,
        table_velocity,
        table_copies,
    )


def solution(mesh):
    in_specs = (
        P("rep", None, "shard", "tp"),
        P("rep", "shard", "tp"),
        P(None, "shard", None),
        P(None, "shard", None),
        P("shard", None),
        P("shard", None),
    )
    out_specs = (
        P(None, "shard", None),
        P(None, "shard", None),
        P(None, "shard", "tp"),
        P("shard", None),
        P("shard", None),
        P("shard", "tp"),
    )
    return jax.shard_map(local, mesh=mesh, in_specs=in_specs, out_specs=out_specs, check_vma=False)
```

```python
import jax
import jax.numpy as jnp
from jax import lax
from jax.sharding import PartitionSpec as P
from jax.experimental import pallas as pl
from jax.experimental.pallas import tpu as pltpu

momentum_coef = 0.9
outer_rate = 0.7


def update(master, moment, mean):
    velocity = momentum_coef * moment + mean
    weights = master - outer_rate * (mean + momentum_coef * velocity)
    return weights, velocity


def pairs(n, flip):
    return [(i, i ^ flip) for i in range(n)]


def rep_scatter(x):
    r = lax.axis_index("rep")
    n = lax.axis_size("rep")
    core, x_lo = r % 2, r // 2
    x4 = x.reshape(2, 2, -1)
    mine = lax.dynamic_index_in_dim(x4, core, 1, keepdims=False)
    other = lax.dynamic_index_in_dim(x4, 1 - core, 1, keepdims=False)
    a = mine + lax.ppermute(other, "rep", pairs(n, 1))
    keep = lax.dynamic_index_in_dim(a, x_lo, 0, keepdims=False)
    send = lax.dynamic_index_in_dim(a, 1 - x_lo, 0, keepdims=False)
    return keep + lax.ppermute(send, "rep", pairs(n, 2))


def rep_gather(x):
    r = lax.axis_index("rep")
    n = lax.axis_size("rep")
    core, x_lo = r % 2, r // 2
    cross = lax.ppermute(x, "rep", pairs(n, 2))
    pair = jax.tree.map(
        lambda a, b: jnp.where(x_lo == 0, jnp.stack([a, b]), jnp.stack([b, a])), x, cross
    )
    sib = lax.ppermute(pair, "rep", pairs(n, 1))
    full = jax.tree.map(
        lambda a, b: jnp.where(core == 0, jnp.stack([a, b], 1), jnp.stack([b, a], 1)), pair, sib
    )
    return jax.tree.map(lambda a, f: f.reshape((n,) + a.shape), x, full)


def gather_pieces(x):
    r = lax.axis_index("rep")
    n = lax.axis_size("rep")
    cross = lax.ppermute(x, "rep", pairs(n, 2))
    sib, sib_cross = lax.ppermute((x, cross), "rep", pairs(n, 1))
    return x, sib, cross, sib_cross


def update_kernel(scale, r_ref, p0, p1, p2, p3, master_ref, moment_ref, w_ref, v_ref):
    p = pl.program_id(0)
    for i, piece in enumerate((p0, p1, p2, p3)):

        @pl.when(p == i)
        def _():
            x = piece[...]
            x = x.reshape(x.shape[0] * x.shape[1], x.shape[2])
            mean = x.T * scale
            weights, velocity = update(
                master_ref[...], moment_ref[...], mean.reshape(master_ref.shape)
            )
            w_ref[...] = weights
            v_ref[...] = velocity


def fused_update(pieces, master, moment, scale):
    srcs, wdt, cols = pieces[0].shape
    lead = master.shape[:-2]
    if lead:
        blk = (1,) * len(lead) + master.shape[-2:]
        idx = lambda p, r_ref: (lax.bitwise_xor(r_ref[0], p), 0, 0)
    else:
        blk = (cols,) + master.shape[-1:]
        idx = lambda p, r_ref: (lax.bitwise_xor(r_ref[0], p), 0)
    big = pl.BlockSpec(blk, idx)
    whole = pl.BlockSpec((srcs, wdt, cols), lambda p, r_ref: (0, 0, 0))
    r = lax.axis_index("rep").astype(jnp.int32).reshape(1)
    return pl.pallas_call(
        lambda *refs: update_kernel(scale, *refs),
        grid_spec=pltpu.PrefetchScalarGridSpec(
            num_scalar_prefetch=1,
            grid=(len(pieces),),
            in_specs=[whole] * len(pieces) + [big, big],
            out_specs=[big, big],
        ),
        out_shape=[
            jax.ShapeDtypeStruct(master.shape, master.dtype),
            jax.ShapeDtypeStruct(master.shape, master.dtype),
        ],
    )(r, *pieces, master, moment)


def local(expert_change, table_change, expert_master, expert_moment, table_master, table_moment):
    groups = lax.axis_size("rep")
    tensor = lax.axis_size("tp")
    shards = lax.axis_size("shard")
    t = lax.axis_index("tp")
    mats, width, half = expert_change.shape[1:]
    rows = expert_master.shape[1]
    vrows = table_master.shape[0]
    per_half = shards // tensor
    sub = vrows // groups
    esize = width * half

    ex = expert_change[0].reshape(mats, esize)
    tx = table_change[0].reshape(width, per_half, groups, sub)
    tx = jnp.transpose(tx, (2, 0, 1, 3)).reshape(groups, -1)
    q = rep_scatter(jnp.concatenate([ex, tx], axis=1))

    other = lax.ppermute(q, "tp", pairs(tensor, 1))
    halves = jnp.where(t == 0, jnp.stack([q, other]), jnp.stack([other, q]))
    he = halves[:, :esize].reshape(tensor, width, per_half, rows)
    he = jnp.transpose(he, (0, 2, 1, 3)).reshape(shards, width * rows)
    ht = halves[:, esize:].reshape(tensor, width, per_half, sub)
    ht = jnp.transpose(ht, (0, 2, 1, 3)).reshape(shards, width * sub)
    got = lax.all_to_all(jnp.concatenate([he, ht], 1), "shard", 0, 0, tiled=True)

    ge = got[:, : width * rows].reshape(shards, width, rows)
    gt = got[:, width * rows :].reshape(shards, width, sub)

    r = lax.axis_index("rep")
    own_e = jnp.transpose(ge.reshape(shards * width, rows)) / groups
    own_e, _ = update(
        lax.dynamic_index_in_dim(expert_master, r, 0, keepdims=False),
        lax.dynamic_index_in_dim(expert_moment, r, 0, keepdims=False),
        own_e,
    )
    le = jnp.transpose(own_e.astype(jnp.bfloat16).reshape(rows, shards, width), (1, 2, 0))
    own_t = jnp.transpose(gt.reshape(shards * width, sub)) / groups
    own_t, _ = update(
        lax.dynamic_slice_in_dim(table_master, r * sub, sub, 0),
        lax.dynamic_slice_in_dim(table_moment, r * sub, sub, 0),
        own_t,
    )
    lt = jnp.transpose(own_t.astype(jnp.bfloat16).reshape(sub, shards, width), (1, 2, 0))
    back = jnp.concatenate([le.reshape(shards, -1), lt.reshape(shards, -1)], 1)
    back = lax.all_to_all(back, "shard", 0, 0, tiled=True)

    pieces_e = gather_pieces(ge)
    pieces_t = gather_pieces(gt)
    expert_weights, expert_velocity = fused_update(
        pieces_e, expert_master, expert_moment, 1.0 / groups
    )
    table_weights, table_velocity = fused_update(
        pieces_t, table_master, table_moment, 1.0 / groups
    )

    back = lax.dynamic_slice_in_dim(back, t * per_half, per_half, 0)
    allq = rep_gather(back)
    ce = allq[:, :, : width * rows].reshape(groups, per_half, width, rows)
    expert_copies = jnp.transpose(ce, (0, 2, 1, 3)).reshape(mats, width, per_half * rows)
    ct = allq[:, :, width * rows :].reshape(groups, per_half, width, sub)
    table_copies = jnp.transpose(ct, (2, 1, 0, 3)).reshape(width, per_half * vrows)
    return (
        expert_weights,
        expert_velocity,
        expert_copies,
        table_weights,
        table_velocity,
        table_copies,
    )


def solution(mesh):
    in_specs = (
        P("rep", None, "shard", "tp"),
        P("rep", "shard", "tp"),
        P(None, "shard", None),
        P(None, "shard", None),
        P("shard", None),
        P("shard", None),
    )
    out_specs = (
        P(None, "shard", None),
        P(None, "shard", None),
        P(None, "shard", "tp"),
        P("shard", None),
        P("shard", None),
        P("shard", "tp"),
    )
    return jax.shard_map(local, mesh=mesh, in_specs=in_specs, out_specs=out_specs, check_vma=False)
```

```python
import jax
import jax.numpy as jnp
from jax import lax
from jax.sharding import PartitionSpec as P
from jax.experimental import pallas as pl
from jax.experimental.pallas import tpu as pltpu

momentum_coef = 0.9
outer_rate = 0.7


def update(master, moment, mean):
    velocity = momentum_coef * moment + mean
    weights = master - outer_rate * (mean + momentum_coef * velocity)
    return weights, velocity


def pairs(n, flip):
    return [(i, i ^ flip) for i in range(n)]


def rep_scatter(x):
    r = lax.axis_index("rep")
    n = lax.axis_size("rep")
    core, x_lo = r % 2, r // 2
    x4 = x.reshape(2, 2, -1)
    mine = lax.dynamic_index_in_dim(x4, core, 1, keepdims=False)
    other = lax.dynamic_index_in_dim(x4, 1 - core, 1, keepdims=False)
    a = mine + lax.ppermute(other, "rep", pairs(n, 1))
    keep = lax.dynamic_index_in_dim(a, x_lo, 0, keepdims=False)
    send = lax.dynamic_index_in_dim(a, 1 - x_lo, 0, keepdims=False)
    return keep + lax.ppermute(send, "rep", pairs(n, 2))


def rep_gather(x):
    r = lax.axis_index("rep")
    n = lax.axis_size("rep")
    core, x_lo = r % 2, r // 2
    cross = lax.ppermute(x, "rep", pairs(n, 2))
    pair = jax.tree.map(
        lambda a, b: jnp.where(x_lo == 0, jnp.stack([a, b]), jnp.stack([b, a])), x, cross
    )
    sib = lax.ppermute(pair, "rep", pairs(n, 1))
    full = jax.tree.map(
        lambda a, b: jnp.where(core == 0, jnp.stack([a, b], 1), jnp.stack([b, a], 1)), pair, sib
    )
    return jax.tree.map(lambda a, f: f.reshape((n,) + a.shape), x, full)


def gather_pieces(x):
    r = lax.axis_index("rep")
    n = lax.axis_size("rep")
    sib = lax.ppermute(x, "rep", pairs(n, 1))
    cross = lax.ppermute(x, "rep", pairs(n, 2))
    sib_cross = lax.ppermute(cross, "rep", pairs(n, 1))
    return x, sib, cross, sib_cross


def update_kernel(scale, count, r_ref, *refs):
    pieces = refs[:count]
    master_ref, moment_ref = refs[count : count + 2]
    w_ref, v_ref = refs[-2:]
    p = pl.program_id(0)
    for i, piece in enumerate(pieces):

        @pl.when(p == i)
        def _():
            x = piece[...]
            x = x.reshape(x.shape[0] * x.shape[1], x.shape[2])
            mean = x.T * scale
            weights, velocity = update(
                master_ref[...], moment_ref[...], mean.reshape(master_ref.shape)
            )
            w_ref[...] = weights
            v_ref[...] = velocity


def fused_update(pieces, first, master, moment, scale, into=None):
    srcs, wdt, cols = pieces[0].shape
    count = len(pieces)
    lead = master.shape[:-2]
    if lead:
        blk = (1,) * len(lead) + master.shape[-2:]
        idx = lambda p, r_ref: (lax.bitwise_xor(r_ref[0], p + first), 0, 0)
    else:
        blk = (cols,) + master.shape[-1:]
        idx = lambda p, r_ref: (lax.bitwise_xor(r_ref[0], p + first), 0)
    big = pl.BlockSpec(blk, idx)
    whole = pl.BlockSpec((srcs, wdt, cols), lambda p, r_ref: (0, 0, 0))
    r = lax.axis_index("rep").astype(jnp.int32).reshape(1)
    args = [r, *pieces, master, moment]
    in_specs = [whole] * count + [big, big]
    aliases = {}
    if into is not None:
        aliases = {len(args): 0, len(args) + 1: 1}
        args += list(into)
        in_specs += [pl.BlockSpec(memory_space=pl.ANY)] * 2
    return pl.pallas_call(
        lambda *refs: update_kernel(scale, count, *refs),
        grid_spec=pltpu.PrefetchScalarGridSpec(
            num_scalar_prefetch=1,
            grid=(count,),
            in_specs=in_specs,
            out_specs=[big, big],
        ),
        out_shape=[
            jax.ShapeDtypeStruct(master.shape, master.dtype),
            jax.ShapeDtypeStruct(master.shape, master.dtype),
        ],
        input_output_aliases=aliases,
    )(*args)


def local(expert_change, table_change, expert_master, expert_moment, table_master, table_moment):
    groups = lax.axis_size("rep")
    tensor = lax.axis_size("tp")
    shards = lax.axis_size("shard")
    t = lax.axis_index("tp")
    mats, width, half = expert_change.shape[1:]
    rows = expert_master.shape[1]
    vrows = table_master.shape[0]
    per_half = shards // tensor
    sub = vrows // groups
    esize = width * half

    ex = expert_change[0].reshape(mats, esize)
    tx = table_change[0].reshape(width, per_half, groups, sub)
    tx = jnp.transpose(tx, (2, 0, 1, 3)).reshape(groups, -1)
    q = rep_scatter(jnp.concatenate([ex, tx], axis=1))

    other = lax.ppermute(q, "tp", pairs(tensor, 1))
    halves = jnp.where(t == 0, jnp.stack([q, other]), jnp.stack([other, q]))
    he = halves[:, :esize].reshape(tensor, width, per_half, rows)
    he = jnp.transpose(he, (0, 2, 1, 3)).reshape(shards, width * rows)
    ht = halves[:, esize:].reshape(tensor, width, per_half, sub)
    ht = jnp.transpose(ht, (0, 2, 1, 3)).reshape(shards, width * sub)
    got = lax.all_to_all(jnp.concatenate([he, ht], 1), "shard", 0, 0, tiled=True)

    ge = got[:, : width * rows].reshape(shards, width, rows)
    gt = got[:, width * rows :].reshape(shards, width, sub)

    r = lax.axis_index("rep")
    own_e = jnp.transpose(ge.reshape(shards * width, rows)) / groups
    own_e, _ = update(
        lax.dynamic_index_in_dim(expert_master, r, 0, keepdims=False),
        lax.dynamic_index_in_dim(expert_moment, r, 0, keepdims=False),
        own_e,
    )
    le = jnp.transpose(own_e.astype(jnp.bfloat16).reshape(rows, shards, width), (1, 2, 0))
    own_t = jnp.transpose(gt.reshape(shards * width, sub)) / groups
    own_t, _ = update(
        lax.dynamic_slice_in_dim(table_master, r * sub, sub, 0),
        lax.dynamic_slice_in_dim(table_moment, r * sub, sub, 0),
        own_t,
    )
    lt = jnp.transpose(own_t.astype(jnp.bfloat16).reshape(sub, shards, width), (1, 2, 0))
    back = jnp.concatenate([le.reshape(shards, -1), lt.reshape(shards, -1)], 1)
    back = lax.all_to_all(back, "shard", 0, 0, tiled=True)

    pieces_e = gather_pieces(ge)
    pieces_t = gather_pieces(gt)
    scale = 1.0 / groups
    early_e = fused_update(pieces_e[:2], 0, expert_master, expert_moment, scale)
    early_t = fused_update(pieces_t[:2], 0, table_master, table_moment, scale)
    expert_weights, expert_velocity = fused_update(
        pieces_e[2:], 2, expert_master, expert_moment, scale, early_e
    )
    table_weights, table_velocity = fused_update(
        pieces_t[2:], 2, table_master, table_moment, scale, early_t
    )

    back = lax.dynamic_slice_in_dim(back, t * per_half, per_half, 0)
    allq = rep_gather(back)
    ce = allq[:, :, : width * rows].reshape(groups, per_half, width, rows)
    expert_copies = jnp.transpose(ce, (0, 2, 1, 3)).reshape(mats, width, per_half * rows)
    ct = allq[:, :, width * rows :].reshape(groups, per_half, width, sub)
    table_copies = jnp.transpose(ct, (2, 1, 0, 3)).reshape(width, per_half * vrows)
    return (
        expert_weights,
        expert_velocity,
        expert_copies,
        table_weights,
        table_velocity,
        table_copies,
    )


def solution(mesh):
    in_specs = (
        P("rep", None, "shard", "tp"),
        P("rep", "shard", "tp"),
        P(None, "shard", None),
        P(None, "shard", None),
        P("shard", None),
        P("shard", None),
    )
    out_specs = (
        P(None, "shard", None),
        P(None, "shard", None),
        P(None, "shard", "tp"),
        P("shard", None),
        P("shard", None),
        P("shard", "tp"),
    )
    return jax.shard_map(local, mesh=mesh, in_specs=in_specs, out_specs=out_specs, check_vma=False)
```

```python
import jax
import jax.numpy as jnp
from jax import lax
from jax.sharding import PartitionSpec as P
from jax.experimental import pallas as pl
from jax.experimental.pallas import tpu as pltpu

momentum_coef = 0.9
outer_rate = 0.7


def update(master, moment, mean):
    velocity = momentum_coef * moment + mean
    weights = master - outer_rate * (mean + momentum_coef * velocity)
    return weights, velocity


def pairs(n, flip):
    return [(i, i ^ flip) for i in range(n)]


def rep_scatter(x):
    r = lax.axis_index("rep")
    n = lax.axis_size("rep")
    core, x_lo = r % 2, r // 2
    x4 = jax.tree.map(lambda a: a.reshape(2, 2, -1), x)
    pick = lambda tree, i, axis: jax.tree.map(
        lambda a: lax.dynamic_index_in_dim(a, i, axis, keepdims=False), tree
    )
    got = lax.ppermute(pick(x4, 1 - core, 1), "rep", pairs(n, 1))
    a = jax.tree.map(jnp.add, pick(x4, core, 1), got)
    got = lax.ppermute(pick(a, 1 - x_lo, 0), "rep", pairs(n, 2))
    return jax.tree.map(jnp.add, pick(a, x_lo, 0), got)


def rep_gather(x):
    r = lax.axis_index("rep")
    n = lax.axis_size("rep")
    core, x_lo = r % 2, r // 2
    cross = lax.ppermute(x, "rep", pairs(n, 2))
    pair = jax.tree.map(
        lambda a, b: jnp.where(x_lo == 0, jnp.stack([a, b]), jnp.stack([b, a])), x, cross
    )
    sib = lax.ppermute(pair, "rep", pairs(n, 1))
    full = jax.tree.map(
        lambda a, b: jnp.where(core == 0, jnp.stack([a, b], 1), jnp.stack([b, a], 1)), pair, sib
    )
    return jax.tree.map(lambda a, f: f.reshape((n,) + a.shape), x, full)


def gather_pieces(x):
    r = lax.axis_index("rep")
    n = lax.axis_size("rep")
    cross = lax.ppermute(x, "rep", pairs(n, 2))
    sib, sib_cross = lax.ppermute((x, cross), "rep", pairs(n, 1))
    return x, sib, cross, sib_cross


def update_kernel(scale, r_ref, p0, p1, p2, p3, master_ref, moment_ref, w_ref, v_ref):
    p = pl.program_id(0)
    for i, piece in enumerate((p0, p1, p2, p3)):

        @pl.when(p == i)
        def _():
            x = piece[...]
            x = x.reshape(x.shape[0] * x.shape[1], x.shape[2])
            mean = x.T * scale
            weights, velocity = update(
                master_ref[...], moment_ref[...], mean.reshape(master_ref.shape)
            )
            w_ref[...] = weights
            v_ref[...] = velocity


def fused_update(pieces, master, moment, scale):
    srcs, wdt, cols = pieces[0].shape
    lead = master.shape[:-2]
    if lead:
        blk = (1,) * len(lead) + master.shape[-2:]
        idx = lambda p, r_ref: (lax.bitwise_xor(r_ref[0], p), 0, 0)
    else:
        blk = (cols,) + master.shape[-1:]
        idx = lambda p, r_ref: (lax.bitwise_xor(r_ref[0], p), 0)
    big = pl.BlockSpec(blk, idx)
    whole = pl.BlockSpec((srcs, wdt, cols), lambda p, r_ref: (0, 0, 0))
    r = lax.axis_index("rep").astype(jnp.int32).reshape(1)
    return pl.pallas_call(
        lambda *refs: update_kernel(scale, *refs),
        grid_spec=pltpu.PrefetchScalarGridSpec(
            num_scalar_prefetch=1,
            grid=(len(pieces),),
            in_specs=[whole] * len(pieces) + [big, big],
            out_specs=[big, big],
        ),
        out_shape=[
            jax.ShapeDtypeStruct(master.shape, master.dtype),
            jax.ShapeDtypeStruct(master.shape, master.dtype),
        ],
    )(r, *pieces, master, moment)


def local(expert_change, table_change, expert_master, expert_moment, table_master, table_moment):
    groups = lax.axis_size("rep")
    tensor = lax.axis_size("tp")
    shards = lax.axis_size("shard")
    t = lax.axis_index("tp")
    mats, width, half = expert_change.shape[1:]
    rows = expert_master.shape[1]
    vrows = table_master.shape[0]
    per_half = shards // tensor
    sub = vrows // groups
    esize = width * half

    ex = expert_change[0].reshape(mats, esize)
    tx = table_change[0].reshape(width, per_half, groups, sub)
    tx = jnp.transpose(tx, (2, 0, 1, 3)).reshape(groups, -1)
    q = rep_scatter((ex, tx))

    other = lax.ppermute(q, "tp", pairs(tensor, 1))
    halves = jax.tree.map(
        lambda a, b: jnp.where(t == 0, jnp.stack([a, b]), jnp.stack([b, a])), q, other
    )
    he = halves[0].reshape(tensor, width, per_half, rows)
    he = jnp.transpose(he, (0, 2, 1, 3)).reshape(shards, width * rows)
    ht = halves[1].reshape(tensor, width, per_half, sub)
    ht = jnp.transpose(ht, (0, 2, 1, 3)).reshape(shards, width * sub)
    got = lax.all_to_all(jnp.concatenate([he, ht], 1), "shard", 0, 0, tiled=True)

    ge = got[:, : width * rows].reshape(shards, width, rows)
    gt = got[:, width * rows :].reshape(shards, width, sub)

    r = lax.axis_index("rep")
    own_e = jnp.transpose(ge.reshape(shards * width, rows)) / groups
    own_e, _ = update(
        lax.dynamic_index_in_dim(expert_master, r, 0, keepdims=False),
        lax.dynamic_index_in_dim(expert_moment, r, 0, keepdims=False),
        own_e,
    )
    le = jnp.transpose(own_e.astype(jnp.bfloat16).reshape(rows, shards, width), (1, 2, 0))
    own_t = jnp.transpose(gt.reshape(shards * width, sub)) / groups
    own_t, _ = update(
        lax.dynamic_slice_in_dim(table_master, r * sub, sub, 0),
        lax.dynamic_slice_in_dim(table_moment, r * sub, sub, 0),
        own_t,
    )
    lt = jnp.transpose(own_t.astype(jnp.bfloat16).reshape(sub, shards, width), (1, 2, 0))
    back = jnp.concatenate([le.reshape(shards, -1), lt.reshape(shards, -1)], 1)
    back = lax.all_to_all(back, "shard", 0, 0, tiled=True)

    pieces_e = gather_pieces(ge)
    pieces_t = gather_pieces(gt)
    expert_weights, expert_velocity = fused_update(
        pieces_e, expert_master, expert_moment, 1.0 / groups
    )
    table_weights, table_velocity = fused_update(
        pieces_t, table_master, table_moment, 1.0 / groups
    )

    back = lax.dynamic_slice_in_dim(back, t * per_half, per_half, 0)
    allq = rep_gather(back)
    ce = allq[:, :, : width * rows].reshape(groups, per_half, width, rows)
    expert_copies = jnp.transpose(ce, (0, 2, 1, 3)).reshape(mats, width, per_half * rows)
    ct = allq[:, :, width * rows :].reshape(groups, per_half, width, sub)
    table_copies = jnp.transpose(ct, (2, 1, 0, 3)).reshape(width, per_half * vrows)
    return (
        expert_weights,
        expert_velocity,
        expert_copies,
        table_weights,
        table_velocity,
        table_copies,
    )


def solution(mesh):
    in_specs = (
        P("rep", None, "shard", "tp"),
        P("rep", "shard", "tp"),
        P(None, "shard", None),
        P(None, "shard", None),
        P("shard", None),
        P("shard", None),
    )
    out_specs = (
        P(None, "shard", None),
        P(None, "shard", None),
        P(None, "shard", "tp"),
        P("shard", None),
        P("shard", None),
        P("shard", "tp"),
    )
    return jax.shard_map(local, mesh=mesh, in_specs=in_specs, out_specs=out_specs, check_vma=False)
```

```python
import jax
import jax.numpy as jnp
from jax import lax
from jax.sharding import PartitionSpec as P
from jax.experimental import pallas as pl
from jax.experimental.pallas import tpu as pltpu

momentum_coef = 0.9
outer_rate = 0.7


def update(master, moment, mean):
    velocity = momentum_coef * moment + mean
    weights = master - outer_rate * (mean + momentum_coef * velocity)
    return weights, velocity


def pairs(n, flip):
    return [(i, i ^ flip) for i in range(n)]


def rep_scatter(x):
    r = lax.axis_index("rep")
    n = lax.axis_size("rep")
    core, x_lo = r % 2, r // 2
    x4 = jax.tree.map(lambda a: a.reshape(2, 2, -1), x)
    pick = lambda tree, i, axis: jax.tree.map(
        lambda a: lax.dynamic_index_in_dim(a, i, axis, keepdims=False), tree
    )
    got = lax.ppermute(pick(x4, 1 - core, 1), "rep", pairs(n, 1))
    a = jax.tree.map(jnp.add, pick(x4, core, 1), got)
    got = lax.ppermute(pick(a, 1 - x_lo, 0), "rep", pairs(n, 2))
    return jax.tree.map(jnp.add, pick(a, x_lo, 0), got)


def rep_gather(x):
    r = lax.axis_index("rep")
    n = lax.axis_size("rep")
    core, x_lo = r % 2, r // 2
    cross = lax.ppermute(x, "rep", pairs(n, 2))
    pair = jax.tree.map(
        lambda a, b: jnp.where(x_lo == 0, jnp.stack([a, b]), jnp.stack([b, a])), x, cross
    )
    sib = lax.ppermute(pair, "rep", pairs(n, 1))
    full = jax.tree.map(
        lambda a, b: jnp.where(core == 0, jnp.stack([a, b], 1), jnp.stack([b, a], 1)), pair, sib
    )
    return jax.tree.map(lambda a, f: f.reshape((n,) + a.shape), x, full)


def gather_pieces(x):
    r = lax.axis_index("rep")
    n = lax.axis_size("rep")
    cross = lax.ppermute(x, "rep", pairs(n, 2))
    sib, sib_cross = lax.ppermute((x, cross), "rep", pairs(n, 1))
    return x, sib, cross, sib_cross


def update_kernel(scale, r_ref, p0, p1, p2, p3, master_ref, moment_ref, w_ref, v_ref):
    p = pl.program_id(0)
    for i, piece in enumerate((p0, p1, p2, p3)):

        @pl.when(p == i)
        def _():
            x = piece[...]
            x = x.reshape(x.shape[0] * x.shape[1], x.shape[2])
            mean = x.T * scale
            weights, velocity = update(
                master_ref[...], moment_ref[...], mean.reshape(master_ref.shape)
            )
            w_ref[...] = weights
            v_ref[...] = velocity


def fused_update(pieces, master, moment, scale):
    srcs, wdt, cols = pieces[0].shape
    lead = master.shape[:-2]
    if lead:
        blk = (1,) * len(lead) + master.shape[-2:]
        idx = lambda p, r_ref: (lax.bitwise_xor(r_ref[0], p), 0, 0)
    else:
        blk = (cols,) + master.shape[-1:]
        idx = lambda p, r_ref: (lax.bitwise_xor(r_ref[0], p), 0)
    big = pl.BlockSpec(blk, idx)
    whole = pl.BlockSpec((srcs, wdt, cols), lambda p, r_ref: (0, 0, 0))
    r = lax.axis_index("rep").astype(jnp.int32).reshape(1)
    return pl.pallas_call(
        lambda *refs: update_kernel(scale, *refs),
        grid_spec=pltpu.PrefetchScalarGridSpec(
            num_scalar_prefetch=1,
            grid=(len(pieces),),
            in_specs=[whole] * len(pieces) + [big, big],
            out_specs=[big, big],
        ),
        out_shape=[
            jax.ShapeDtypeStruct(master.shape, master.dtype),
            jax.ShapeDtypeStruct(master.shape, master.dtype),
        ],
    )(r, *pieces, master, moment)


def local(expert_change, table_change, expert_master, expert_moment, table_master, table_moment):
    groups = lax.axis_size("rep")
    tensor = lax.axis_size("tp")
    shards = lax.axis_size("shard")
    t = lax.axis_index("tp")
    mats, width, half = expert_change.shape[1:]
    rows = expert_master.shape[1]
    vrows = table_master.shape[0]
    per_half = shards // tensor
    sub = vrows // groups
    esize = width * half

    ex = expert_change[0].reshape(mats, esize)
    tx = table_change[0].reshape(width, per_half, groups, sub)
    tx = jnp.transpose(tx, (2, 0, 1, 3)).reshape(groups, -1)
    q = rep_scatter((ex, tx))

    other = lax.ppermute(q, "tp", pairs(tensor, 1))
    halves = jax.tree.map(
        lambda a, b: jnp.where(t == 0, jnp.stack([a, b]), jnp.stack([b, a])), q, other
    )
    he = halves[0].reshape(tensor, width, per_half, rows)
    he = jnp.transpose(he, (0, 2, 1, 3)).reshape(shards, width * rows)
    ht = halves[1].reshape(tensor, width, per_half, sub)
    ht = jnp.transpose(ht, (0, 2, 1, 3)).reshape(shards, width * sub)
    got = lax.all_to_all(jnp.concatenate([he, ht], 1), "shard", 0, 0, tiled=True)

    ge = got[:, : width * rows].reshape(shards, width, rows)
    gt = got[:, width * rows :].reshape(shards, width, sub)

    r = lax.axis_index("rep")
    own_e = jnp.transpose(ge.reshape(shards * width, rows)) / groups
    own_e, _ = update(
        lax.dynamic_index_in_dim(expert_master, r, 0, keepdims=False),
        lax.dynamic_index_in_dim(expert_moment, r, 0, keepdims=False),
        own_e,
    )
    le = jnp.transpose(own_e.astype(jnp.bfloat16).reshape(rows, shards, width), (1, 2, 0))
    own_t = jnp.transpose(gt.reshape(shards * width, sub)) / groups
    own_t, _ = update(
        lax.dynamic_slice_in_dim(table_master, r * sub, sub, 0),
        lax.dynamic_slice_in_dim(table_moment, r * sub, sub, 0),
        own_t,
    )
    lt = jnp.transpose(own_t.astype(jnp.bfloat16).reshape(sub, shards, width), (1, 2, 0))
    back = jnp.concatenate([le.reshape(shards, -1), lt.reshape(shards, -1)], 1)
    back = lax.all_to_all(back, "shard", 0, 0, tiled=True)

    pieces_e = gather_pieces(ge)
    gt, _ = lax.optimization_barrier((gt, pieces_e[2]))
    pieces_t = gather_pieces(gt)
    expert_weights, expert_velocity = fused_update(
        pieces_e, expert_master, expert_moment, 1.0 / groups
    )
    table_weights, table_velocity = fused_update(
        pieces_t, table_master, table_moment, 1.0 / groups
    )

    back = lax.dynamic_slice_in_dim(back, t * per_half, per_half, 0)
    allq = rep_gather(back)
    ce = allq[:, :, : width * rows].reshape(groups, per_half, width, rows)
    expert_copies = jnp.transpose(ce, (0, 2, 1, 3)).reshape(mats, width, per_half * rows)
    ct = allq[:, :, width * rows :].reshape(groups, per_half, width, sub)
    table_copies = jnp.transpose(ct, (2, 1, 0, 3)).reshape(width, per_half * vrows)
    return (
        expert_weights,
        expert_velocity,
        expert_copies,
        table_weights,
        table_velocity,
        table_copies,
    )


def solution(mesh):
    in_specs = (
        P("rep", None, "shard", "tp"),
        P("rep", "shard", "tp"),
        P(None, "shard", None),
        P(None, "shard", None),
        P("shard", None),
        P("shard", None),
    )
    out_specs = (
        P(None, "shard", None),
        P(None, "shard", None),
        P(None, "shard", "tp"),
        P("shard", None),
        P("shard", None),
        P("shard", "tp"),
    )
    return jax.shard_map(local, mesh=mesh, in_specs=in_specs, out_specs=out_specs, check_vma=False)
```

```python
import jax
import jax.numpy as jnp
from jax import lax
from jax.sharding import PartitionSpec as P
from jax.experimental import pallas as pl
from jax.experimental.pallas import tpu as pltpu

momentum_coef = 0.9
outer_rate = 0.7


def update(master, moment, mean):
    velocity = momentum_coef * moment + mean
    weights = master - outer_rate * (mean + momentum_coef * velocity)
    return weights, velocity


def pairs(n, flip):
    return [(i, i ^ flip) for i in range(n)]


def rep_scatter(x):
    r = lax.axis_index("rep")
    n = lax.axis_size("rep")
    core, x_lo = r % 2, r // 2
    x4 = jax.tree.map(lambda a: a.reshape(2, 2, -1), x)
    pick = lambda tree, i, axis: jax.tree.map(
        lambda a: lax.dynamic_index_in_dim(a, i, axis, keepdims=False), tree
    )
    got = lax.ppermute(pick(x4, 1 - core, 1), "rep", pairs(n, 1))
    a = jax.tree.map(jnp.add, pick(x4, core, 1), got)
    got = lax.ppermute(pick(a, 1 - x_lo, 0), "rep", pairs(n, 2))
    return jax.tree.map(jnp.add, pick(a, x_lo, 0), got)


def rep_gather(x):
    r = lax.axis_index("rep")
    n = lax.axis_size("rep")
    core, x_lo = r % 2, r // 2
    cross = lax.ppermute(x, "rep", pairs(n, 2))
    pair = jax.tree.map(
        lambda a, b: jnp.where(x_lo == 0, jnp.stack([a, b]), jnp.stack([b, a])), x, cross
    )
    sib = lax.ppermute(pair, "rep", pairs(n, 1))
    full = jax.tree.map(
        lambda a, b: jnp.where(core == 0, jnp.stack([a, b], 1), jnp.stack([b, a], 1)), pair, sib
    )
    return jax.tree.map(lambda a, f: f.reshape((n,) + a.shape), x, full)


def gather_pieces(x):
    r = lax.axis_index("rep")
    n = lax.axis_size("rep")
    cross = lax.ppermute(x, "rep", pairs(n, 2))
    sib, sib_cross = lax.ppermute((x, cross), "rep", pairs(n, 1))
    return x, sib, cross, sib_cross


def update_kernel(scale, r_ref, p0, p1, p2, p3, master_ref, moment_ref, w_ref, v_ref):
    p = pl.program_id(0)
    for i, piece in enumerate((p0, p1, p2, p3)):

        @pl.when(p == i)
        def _():
            x = piece[...]
            x = x.reshape(x.shape[0] * x.shape[1], x.shape[2])
            mean = x.T * scale
            weights, velocity = update(
                master_ref[...], moment_ref[...], mean.reshape(master_ref.shape)
            )
            w_ref[...] = weights
            v_ref[...] = velocity


def fused_update(pieces, master, moment, scale):
    srcs, wdt, cols = pieces[0].shape
    lead = master.shape[:-2]
    if lead:
        blk = (1,) * len(lead) + master.shape[-2:]
        idx = lambda p, r_ref: (lax.bitwise_xor(r_ref[0], p), 0, 0)
    else:
        blk = (cols,) + master.shape[-1:]
        idx = lambda p, r_ref: (lax.bitwise_xor(r_ref[0], p), 0)
    big = pl.BlockSpec(blk, idx)
    whole = pl.BlockSpec((srcs, wdt, cols), lambda p, r_ref: (0, 0, 0))
    r = lax.axis_index("rep").astype(jnp.int32).reshape(1)
    return pl.pallas_call(
        lambda *refs: update_kernel(scale, *refs),
        grid_spec=pltpu.PrefetchScalarGridSpec(
            num_scalar_prefetch=1,
            grid=(len(pieces),),
            in_specs=[whole] * len(pieces) + [big, big],
            out_specs=[big, big],
        ),
        out_shape=[
            jax.ShapeDtypeStruct(master.shape, master.dtype),
            jax.ShapeDtypeStruct(master.shape, master.dtype),
        ],
    )(r, *pieces, master, moment)


def local(expert_change, table_change, expert_master, expert_moment, table_master, table_moment):
    groups = lax.axis_size("rep")
    tensor = lax.axis_size("tp")
    shards = lax.axis_size("shard")
    t = lax.axis_index("tp")
    mats, width, half = expert_change.shape[1:]
    rows = expert_master.shape[1]
    vrows = table_master.shape[0]
    per_half = shards // tensor
    sub = vrows // groups
    esize = width * half

    ex = expert_change[0].reshape(mats, esize)
    tx = table_change[0].reshape(width, per_half, groups, sub)
    tx = jnp.transpose(tx, (2, 0, 1, 3)).reshape(groups, -1)
    q = rep_scatter((ex, tx))

    other = lax.ppermute(q, "tp", pairs(tensor, 1))
    halves = jax.tree.map(
        lambda a, b: jnp.where(t == 0, jnp.stack([a, b]), jnp.stack([b, a])), q, other
    )
    he = halves[0].reshape(tensor, width, per_half, rows)
    he = jnp.transpose(he, (0, 2, 1, 3)).reshape(shards, width * rows)
    ht = halves[1].reshape(tensor, width, per_half, sub)
    ht = jnp.transpose(ht, (0, 2, 1, 3)).reshape(shards, width * sub)
    got = lax.all_to_all(jnp.concatenate([he, ht], 1), "shard", 0, 0, tiled=True)

    ge = got[:, : width * rows].reshape(shards, width, rows)
    gt = got[:, width * rows :].reshape(shards, width, sub)

    r = lax.axis_index("rep")
    own_e = jnp.transpose(ge.reshape(shards * width, rows)) / groups
    own_e, _ = update(
        lax.dynamic_index_in_dim(expert_master, r, 0, keepdims=False),
        lax.dynamic_index_in_dim(expert_moment, r, 0, keepdims=False),
        own_e,
    )
    le = jnp.transpose(own_e.astype(jnp.bfloat16).reshape(rows, shards, width), (1, 2, 0))
    own_t = jnp.transpose(gt.reshape(shards * width, sub)) / groups
    own_t, _ = update(
        lax.dynamic_slice_in_dim(table_master, r * sub, sub, 0),
        lax.dynamic_slice_in_dim(table_moment, r * sub, sub, 0),
        own_t,
    )
    lt = jnp.transpose(own_t.astype(jnp.bfloat16).reshape(sub, shards, width), (1, 2, 0))
    back = jnp.concatenate([le.reshape(shards, -1), lt.reshape(shards, -1)], 1)
    back = lax.all_to_all(back, "shard", 0, 0, tiled=True)

    pieces_e = gather_pieces(ge)
    gt, _ = lax.optimization_barrier((gt, pieces_e[2]))
    pieces_t = gather_pieces(gt)
    expert_weights, expert_velocity = fused_update(
        pieces_e, expert_master, expert_moment, 1.0 / groups
    )

    back = lax.dynamic_slice_in_dim(back, t * per_half, per_half, 0)
    allq = rep_gather(back)
    ce = allq[:, :, : width * rows].reshape(groups, per_half, width, rows)
    expert_copies = jnp.transpose(ce, (0, 2, 1, 3)).reshape(mats, width, per_half * rows)
    ct = allq[:, :, width * rows :].reshape(groups, per_half, width, sub)
    table_copies = jnp.transpose(ct, (2, 1, 0, 3)).reshape(width, per_half * vrows)
    pieces_t, expert_copies, table_copies = lax.optimization_barrier(
        (pieces_t, expert_copies, table_copies)
    )
    table_weights, table_velocity = fused_update(
        pieces_t, table_master, table_moment, 1.0 / groups
    )
    return (
        expert_weights,
        expert_velocity,
        expert_copies,
        table_weights,
        table_velocity,
        table_copies,
    )


def solution(mesh):
    in_specs = (
        P("rep", None, "shard", "tp"),
        P("rep", "shard", "tp"),
        P(None, "shard", None),
        P(None, "shard", None),
        P("shard", None),
        P("shard", None),
    )
    out_specs = (
        P(None, "shard", None),
        P(None, "shard", None),
        P(None, "shard", "tp"),
        P("shard", None),
        P("shard", None),
        P("shard", "tp"),
    )
    return jax.shard_map(local, mesh=mesh, in_specs=in_specs, out_specs=out_specs, check_vma=False)
```

```python
import jax
import jax.numpy as jnp
from jax import lax
from jax.sharding import PartitionSpec as P
from jax.experimental import pallas as pl
from jax.experimental.pallas import tpu as pltpu

momentum_coef = 0.9
outer_rate = 0.7


def update(master, moment, mean):
    velocity = momentum_coef * moment + mean
    weights = master - outer_rate * (mean + momentum_coef * velocity)
    return weights, velocity


def pairs(n, flip):
    return [(i, i ^ flip) for i in range(n)]


def rep_scatter(x):
    r = lax.axis_index("rep")
    n = lax.axis_size("rep")
    core, x_lo = r % 2, r // 2
    x4 = jax.tree.map(lambda a: a.reshape(2, 2, -1), x)
    pick = lambda tree, i, axis: jax.tree.map(
        lambda a: lax.dynamic_index_in_dim(a, i, axis, keepdims=False), tree
    )
    got = lax.ppermute(pick(x4, 1 - core, 1), "rep", pairs(n, 1))
    a = jax.tree.map(jnp.add, pick(x4, core, 1), got)
    got = lax.ppermute(pick(a, 1 - x_lo, 0), "rep", pairs(n, 2))
    return jax.tree.map(jnp.add, pick(a, x_lo, 0), got)


def rep_gather(x):
    r = lax.axis_index("rep")
    n = lax.axis_size("rep")
    core, x_lo = r % 2, r // 2
    cross = lax.ppermute(x, "rep", pairs(n, 2))
    pair = jax.tree.map(
        lambda a, b: jnp.where(x_lo == 0, jnp.stack([a, b]), jnp.stack([b, a])), x, cross
    )
    sib = lax.ppermute(pair, "rep", pairs(n, 1))
    full = jax.tree.map(
        lambda a, b: jnp.where(core == 0, jnp.stack([a, b], 1), jnp.stack([b, a], 1)), pair, sib
    )
    return jax.tree.map(lambda a, f: f.reshape((n,) + a.shape), x, full)


def gather_pieces(x):
    r = lax.axis_index("rep")
    n = lax.axis_size("rep")
    sib = lax.ppermute(x, "rep", pairs(n, 1))
    cross = lax.ppermute(x, "rep", pairs(n, 2))
    sib_cross = lax.ppermute(cross, "rep", pairs(n, 1))
    return x, sib, cross, sib_cross


def update_kernel(scale, count, r_ref, *refs):
    pieces = refs[:count]
    master_ref, moment_ref = refs[count : count + 2]
    w_ref, v_ref = refs[-2:]
    p = pl.program_id(0)
    for i, piece in enumerate(pieces):

        @pl.when(p == i)
        def _():
            x = piece[...]
            x = x.reshape(x.shape[0] * x.shape[1], x.shape[2])
            mean = x.T * scale
            weights, velocity = update(
                master_ref[...], moment_ref[...], mean.reshape(master_ref.shape)
            )
            w_ref[...] = weights
            v_ref[...] = velocity


def fused_update(pieces, first, master, moment, scale, into=None):
    srcs, wdt, cols = pieces[0].shape
    count = len(pieces)
    lead = master.shape[:-2]
    if lead:
        blk = (1,) * len(lead) + master.shape[-2:]
        idx = lambda p, r_ref: (lax.bitwise_xor(r_ref[0], p + first), 0, 0)
    else:
        blk = (cols,) + master.shape[-1:]
        idx = lambda p, r_ref: (lax.bitwise_xor(r_ref[0], p + first), 0)
    big = pl.BlockSpec(blk, idx)
    whole = pl.BlockSpec((srcs, wdt, cols), lambda p, r_ref: (0, 0, 0))
    r = lax.axis_index("rep").astype(jnp.int32).reshape(1)
    args = [r, *pieces, master, moment]
    in_specs = [whole] * count + [big, big]
    aliases = {}
    if into is not None:
        aliases = {len(args): 0, len(args) + 1: 1}
        args += list(into)
        in_specs += [pl.BlockSpec(memory_space=pl.ANY)] * 2
    return pl.pallas_call(
        lambda *refs: update_kernel(scale, count, *refs),
        grid_spec=pltpu.PrefetchScalarGridSpec(
            num_scalar_prefetch=1,
            grid=(count,),
            in_specs=in_specs,
            out_specs=[big, big],
        ),
        out_shape=[
            jax.ShapeDtypeStruct(master.shape, master.dtype),
            jax.ShapeDtypeStruct(master.shape, master.dtype),
        ],
        input_output_aliases=aliases,
    )(*args)


def local(expert_change, table_change, expert_master, expert_moment, table_master, table_moment):
    groups = lax.axis_size("rep")
    tensor = lax.axis_size("tp")
    shards = lax.axis_size("shard")
    t = lax.axis_index("tp")
    mats, width, half = expert_change.shape[1:]
    rows = expert_master.shape[1]
    vrows = table_master.shape[0]
    per_half = shards // tensor
    sub = vrows // groups
    esize = width * half

    ex = expert_change[0].reshape(mats, esize)
    tx = table_change[0].reshape(width, per_half, groups, sub)
    tx = jnp.transpose(tx, (2, 0, 1, 3)).reshape(groups, -1)
    q = rep_scatter((ex, tx))

    other = lax.ppermute(q, "tp", pairs(tensor, 1))
    halves = jax.tree.map(
        lambda a, b: jnp.where(t == 0, jnp.stack([a, b]), jnp.stack([b, a])), q, other
    )
    he = halves[0].reshape(tensor, width, per_half, rows)
    he = jnp.transpose(he, (0, 2, 1, 3)).reshape(shards, width * rows)
    ht = halves[1].reshape(tensor, width, per_half, sub)
    ht = jnp.transpose(ht, (0, 2, 1, 3)).reshape(shards, width * sub)
    got = lax.all_to_all(jnp.concatenate([he, ht], 1), "shard", 0, 0, tiled=True)

    ge = got[:, : width * rows].reshape(shards, width, rows)
    gt = got[:, width * rows :].reshape(shards, width, sub)

    r = lax.axis_index("rep")
    own_e = jnp.transpose(ge.reshape(shards * width, rows)) / groups
    own_e, _ = update(
        lax.dynamic_index_in_dim(expert_master, r, 0, keepdims=False),
        lax.dynamic_index_in_dim(expert_moment, r, 0, keepdims=False),
        own_e,
    )
    le = jnp.transpose(own_e.astype(jnp.bfloat16).reshape(rows, shards, width), (1, 2, 0))
    own_t = jnp.transpose(gt.reshape(shards * width, sub)) / groups
    own_t, _ = update(
        lax.dynamic_slice_in_dim(table_master, r * sub, sub, 0),
        lax.dynamic_slice_in_dim(table_moment, r * sub, sub, 0),
        own_t,
    )
    lt = jnp.transpose(own_t.astype(jnp.bfloat16).reshape(sub, shards, width), (1, 2, 0))
    back = jnp.concatenate([le.reshape(shards, -1), lt.reshape(shards, -1)], 1)
    back = lax.all_to_all(back, "shard", 0, 0, tiled=True)

    pieces_e = gather_pieces(ge)
    gt, _ = lax.optimization_barrier((gt, pieces_e[2]))
    pieces_t = gather_pieces(gt)
    scale = 1.0 / groups
    early_e = fused_update(pieces_e[:2], 0, expert_master, expert_moment, scale)
    early_t = fused_update(pieces_t[:2], 0, table_master, table_moment, scale)
    expert_weights, expert_velocity = fused_update(
        pieces_e[2:], 2, expert_master, expert_moment, scale, early_e
    )
    table_weights, table_velocity = fused_update(
        pieces_t[2:], 2, table_master, table_moment, scale, early_t
    )

    back = lax.dynamic_slice_in_dim(back, t * per_half, per_half, 0)
    allq = rep_gather(back)
    ce = allq[:, :, : width * rows].reshape(groups, per_half, width, rows)
    expert_copies = jnp.transpose(ce, (0, 2, 1, 3)).reshape(mats, width, per_half * rows)
    ct = allq[:, :, width * rows :].reshape(groups, per_half, width, sub)
    table_copies = jnp.transpose(ct, (2, 1, 0, 3)).reshape(width, per_half * vrows)
    return (
        expert_weights,
        expert_velocity,
        expert_copies,
        table_weights,
        table_velocity,
        table_copies,
    )


def solution(mesh):
    in_specs = (
        P("rep", None, "shard", "tp"),
        P("rep", "shard", "tp"),
        P(None, "shard", None),
        P(None, "shard", None),
        P("shard", None),
        P("shard", None),
    )
    out_specs = (
        P(None, "shard", None),
        P(None, "shard", None),
        P(None, "shard", "tp"),
        P("shard", None),
        P("shard", None),
        P("shard", "tp"),
    )
    return jax.shard_map(local, mesh=mesh, in_specs=in_specs, out_specs=out_specs, check_vma=False)
```

```python
import jax
import jax.numpy as jnp
from jax import lax
from jax.sharding import PartitionSpec as P
from jax.experimental import pallas as pl
from jax.experimental.pallas import tpu as pltpu

momentum_coef = 0.9
outer_rate = 0.7


def update(master, moment, mean):
    velocity = momentum_coef * moment + mean
    weights = master - outer_rate * (mean + momentum_coef * velocity)
    return weights, velocity


def pairs(n, flip):
    return [(i, i ^ flip) for i in range(n)]


def rep_scatter(x):
    r = lax.axis_index("rep")
    n = lax.axis_size("rep")
    core, x_lo = r % 2, r // 2
    x4 = jax.tree.map(lambda a: a.reshape(2, 2, -1), x)
    pick = lambda tree, i, axis: jax.tree.map(
        lambda a: lax.dynamic_index_in_dim(a, i, axis, keepdims=False), tree
    )
    got = lax.ppermute(pick(x4, 1 - core, 1), "rep", pairs(n, 1))
    a = jax.tree.map(jnp.add, pick(x4, core, 1), got)
    got = lax.ppermute(pick(a, 1 - x_lo, 0), "rep", pairs(n, 2))
    return jax.tree.map(jnp.add, pick(a, x_lo, 0), got)


def rep_gather(x):
    r = lax.axis_index("rep")
    n = lax.axis_size("rep")
    core, x_lo = r % 2, r // 2
    cross = lax.ppermute(x, "rep", pairs(n, 2))
    pair = jax.tree.map(
        lambda a, b: jnp.where(x_lo == 0, jnp.stack([a, b]), jnp.stack([b, a])), x, cross
    )
    sib = lax.ppermute(pair, "rep", pairs(n, 1))
    full = jax.tree.map(
        lambda a, b: jnp.where(core == 0, jnp.stack([a, b], 1), jnp.stack([b, a], 1)), pair, sib
    )
    return jax.tree.map(lambda a, f: f.reshape((n,) + a.shape), x, full)


def gather_pieces(x):
    r = lax.axis_index("rep")
    n = lax.axis_size("rep")
    sib = lax.ppermute(x, "rep", pairs(n, 1))
    cross = lax.ppermute(x, "rep", pairs(n, 2))
    sib_cross = lax.ppermute(cross, "rep", pairs(n, 1))
    return x, sib, cross, sib_cross


def update_kernel(scale, count, r_ref, *refs):
    pieces = refs[:count]
    master_ref, moment_ref = refs[count : count + 2]
    w_ref, v_ref = refs[-2:]
    p = pl.program_id(0)
    for i, piece in enumerate(pieces):

        @pl.when(p == i)
        def _():
            x = piece[...]
            x = x.reshape(x.shape[0] * x.shape[1], x.shape[2])
            mean = x.T * scale
            weights, velocity = update(
                master_ref[...], moment_ref[...], mean.reshape(master_ref.shape)
            )
            w_ref[...] = weights
            v_ref[...] = velocity


def fused_update(pieces, first, master, moment, scale, into=None):
    srcs, wdt, cols = pieces[0].shape
    count = len(pieces)
    lead = master.shape[:-2]
    if lead:
        blk = (1,) * len(lead) + master.shape[-2:]
        idx = lambda p, r_ref: (lax.bitwise_xor(r_ref[0], p + first), 0, 0)
    else:
        blk = (cols,) + master.shape[-1:]
        idx = lambda p, r_ref: (lax.bitwise_xor(r_ref[0], p + first), 0)
    big = pl.BlockSpec(blk, idx)
    whole = pl.BlockSpec((srcs, wdt, cols), lambda p, r_ref: (0, 0, 0))
    r = lax.axis_index("rep").astype(jnp.int32).reshape(1)
    args = [r, *pieces, master, moment]
    in_specs = [whole] * count + [big, big]
    aliases = {}
    if into is not None:
        aliases = {len(args): 0, len(args) + 1: 1}
        args += list(into)
        in_specs += [pl.BlockSpec(memory_space=pl.ANY)] * 2
    return pl.pallas_call(
        lambda *refs: update_kernel(scale, count, *refs),
        grid_spec=pltpu.PrefetchScalarGridSpec(
            num_scalar_prefetch=1,
            grid=(count,),
            in_specs=in_specs,
            out_specs=[big, big],
        ),
        out_shape=[
            jax.ShapeDtypeStruct(master.shape, master.dtype),
            jax.ShapeDtypeStruct(master.shape, master.dtype),
        ],
        input_output_aliases=aliases,
    )(*args)


def local(expert_change, table_change, expert_master, expert_moment, table_master, table_moment):
    groups = lax.axis_size("rep")
    tensor = lax.axis_size("tp")
    shards = lax.axis_size("shard")
    t = lax.axis_index("tp")
    mats, width, half = expert_change.shape[1:]
    rows = expert_master.shape[1]
    vrows = table_master.shape[0]
    per_half = shards // tensor
    sub = vrows // groups
    esize = width * half

    ex = expert_change[0].reshape(mats, esize)
    tx = table_change[0].reshape(width, per_half, groups, sub)
    tx = jnp.transpose(tx, (2, 0, 1, 3)).reshape(groups, -1)
    q = rep_scatter((ex, tx))

    other = lax.ppermute(q, "tp", pairs(tensor, 1))
    halves = jax.tree.map(
        lambda a, b: jnp.where(t == 0, jnp.stack([a, b]), jnp.stack([b, a])), q, other
    )
    he = halves[0].reshape(tensor, width, per_half, rows)
    he = jnp.transpose(he, (0, 2, 1, 3)).reshape(shards, width * rows)
    ht = halves[1].reshape(tensor, width, per_half, sub)
    ht = jnp.transpose(ht, (0, 2, 1, 3)).reshape(shards, width * sub)
    got = lax.all_to_all(jnp.concatenate([he, ht], 1), "shard", 0, 0, tiled=True)

    ge = got[:, : width * rows].reshape(shards, width, rows)
    gt = got[:, width * rows :].reshape(shards, width, sub)

    r = lax.axis_index("rep")
    own_e = jnp.transpose(ge.reshape(shards * width, rows)) / groups
    own_e, _ = update(
        lax.dynamic_index_in_dim(expert_master, r, 0, keepdims=False),
        lax.dynamic_index_in_dim(expert_moment, r, 0, keepdims=False),
        own_e,
    )
    le = jnp.transpose(own_e.astype(jnp.bfloat16).reshape(rows, shards, width), (1, 2, 0))
    own_t = jnp.transpose(gt.reshape(shards * width, sub)) / groups
    own_t, _ = update(
        lax.dynamic_slice_in_dim(table_master, r * sub, sub, 0),
        lax.dynamic_slice_in_dim(table_moment, r * sub, sub, 0),
        own_t,
    )
    lt = jnp.transpose(own_t.astype(jnp.bfloat16).reshape(sub, shards, width), (1, 2, 0))
    back = jnp.concatenate([le.reshape(shards, -1), lt.reshape(shards, -1)], 1)
    back = lax.all_to_all(back, "shard", 0, 0, tiled=True)

    pieces_e = gather_pieces(ge)
    n_rep = lax.axis_size("rep")
    sib_t = lax.ppermute(gt, "rep", pairs(n_rep, 1))
    gt_late, _ = lax.optimization_barrier((gt, pieces_e[2]))
    cross_t = lax.ppermute(gt_late, "rep", pairs(n_rep, 2))
    sib_cross_t = lax.ppermute(cross_t, "rep", pairs(n_rep, 1))
    scale = 1.0 / groups
    early_t = fused_update((gt, sib_t), 0, table_master, table_moment, scale)
    pieces_e, early_t = lax.optimization_barrier((pieces_e, early_t))
    expert_weights, expert_velocity = fused_update(
        pieces_e, 0, expert_master, expert_moment, scale
    )
    table_weights, table_velocity = fused_update(
        (cross_t, sib_cross_t), 2, table_master, table_moment, scale, early_t
    )

    back = lax.dynamic_slice_in_dim(back, t * per_half, per_half, 0)
    allq = rep_gather(back)
    ce = allq[:, :, : width * rows].reshape(groups, per_half, width, rows)
    expert_copies = jnp.transpose(ce, (0, 2, 1, 3)).reshape(mats, width, per_half * rows)
    ct = allq[:, :, width * rows :].reshape(groups, per_half, width, sub)
    table_copies = jnp.transpose(ct, (2, 1, 0, 3)).reshape(width, per_half * vrows)
    return (
        expert_weights,
        expert_velocity,
        expert_copies,
        table_weights,
        table_velocity,
        table_copies,
    )


def solution(mesh):
    in_specs = (
        P("rep", None, "shard", "tp"),
        P("rep", "shard", "tp"),
        P(None, "shard", None),
        P(None, "shard", None),
        P("shard", None),
        P("shard", None),
    )
    out_specs = (
        P(None, "shard", None),
        P(None, "shard", None),
        P(None, "shard", "tp"),
        P("shard", None),
        P("shard", None),
        P("shard", "tp"),
    )
    return jax.shard_map(local, mesh=mesh, in_specs=in_specs, out_specs=out_specs, check_vma=False)
```

```python
import jax
import jax.numpy as jnp
from jax import lax
from jax.sharding import PartitionSpec as P
from jax.experimental import pallas as pl
from jax.experimental.pallas import tpu as pltpu

momentum_coef = 0.9
outer_rate = 0.7


def update(master, moment, mean):
    velocity = momentum_coef * moment + mean
    weights = master - outer_rate * (mean + momentum_coef * velocity)
    return weights, velocity


def pairs(n, flip):
    return [(i, i ^ flip) for i in range(n)]


def rep_scatter(x):
    r = lax.axis_index("rep")
    n = lax.axis_size("rep")
    core, x_lo = r % 2, r // 2
    x4 = jax.tree.map(lambda a: a.reshape(2, 2, -1), x)
    pick = lambda tree, i, axis: jax.tree.map(
        lambda a: lax.dynamic_index_in_dim(a, i, axis, keepdims=False), tree
    )
    got = lax.ppermute(pick(x4, 1 - core, 1), "rep", pairs(n, 1))
    a = jax.tree.map(jnp.add, pick(x4, core, 1), got)
    got = lax.ppermute(pick(a, 1 - x_lo, 0), "rep", pairs(n, 2))
    return jax.tree.map(jnp.add, pick(a, x_lo, 0), got)


def rep_gather(x):
    r = lax.axis_index("rep")
    n = lax.axis_size("rep")
    core, x_lo = r % 2, r // 2
    cross = lax.ppermute(x, "rep", pairs(n, 2))
    pair = jax.tree.map(
        lambda a, b: jnp.where(x_lo == 0, jnp.stack([a, b]), jnp.stack([b, a])), x, cross
    )
    sib = lax.ppermute(pair, "rep", pairs(n, 1))
    full = jax.tree.map(
        lambda a, b: jnp.where(core == 0, jnp.stack([a, b], 1), jnp.stack([b, a], 1)), pair, sib
    )
    return jax.tree.map(lambda a, f: f.reshape((n,) + a.shape), x, full)


def gather_pieces(x):
    r = lax.axis_index("rep")
    n = lax.axis_size("rep")
    sib = lax.ppermute(x, "rep", pairs(n, 1))
    cross = lax.ppermute(x, "rep", pairs(n, 2))
    sib_cross = lax.ppermute(cross, "rep", pairs(n, 1))
    return x, sib, cross, sib_cross


def update_kernel(scale, count, r_ref, *refs):
    pieces = refs[:count]
    master_ref, moment_ref = refs[count : count + 2]
    w_ref, v_ref = refs[-2:]
    p = pl.program_id(0)
    for i, piece in enumerate(pieces):

        @pl.when(p == i)
        def _():
            x = piece[...]
            x = x.reshape(x.shape[0] * x.shape[1], x.shape[2])
            mean = x.T * scale
            weights, velocity = update(
                master_ref[...], moment_ref[...], mean.reshape(master_ref.shape)
            )
            w_ref[...] = weights
            v_ref[...] = velocity


def fused_update(pieces, first, master, moment, scale, into=None):
    srcs, wdt, cols = pieces[0].shape
    count = len(pieces)
    lead = master.shape[:-2]
    if lead:
        blk = (1,) * len(lead) + master.shape[-2:]
        idx = lambda p, r_ref: (lax.bitwise_xor(r_ref[0], p + first), 0, 0)
    else:
        blk = (cols,) + master.shape[-1:]
        idx = lambda p, r_ref: (lax.bitwise_xor(r_ref[0], p + first), 0)
    big = pl.BlockSpec(blk, idx)
    whole = pl.BlockSpec((srcs, wdt, cols), lambda p, r_ref: (0, 0, 0))
    r = lax.axis_index("rep").astype(jnp.int32).reshape(1)
    args = [r, *pieces, master, moment]
    in_specs = [whole] * count + [big, big]
    aliases = {}
    if into is not None:
        aliases = {len(args): 0, len(args) + 1: 1}
        args += list(into)
        in_specs += [pl.BlockSpec(memory_space=pl.ANY)] * 2
    return pl.pallas_call(
        lambda *refs: update_kernel(scale, count, *refs),
        grid_spec=pltpu.PrefetchScalarGridSpec(
            num_scalar_prefetch=1,
            grid=(count,),
            in_specs=in_specs,
            out_specs=[big, big],
        ),
        out_shape=[
            jax.ShapeDtypeStruct(master.shape, master.dtype),
            jax.ShapeDtypeStruct(master.shape, master.dtype),
        ],
        input_output_aliases=aliases,
    )(*args)


def local(expert_change, table_change, expert_master, expert_moment, table_master, table_moment):
    groups = lax.axis_size("rep")
    tensor = lax.axis_size("tp")
    shards = lax.axis_size("shard")
    t = lax.axis_index("tp")
    mats, width, half = expert_change.shape[1:]
    rows = expert_master.shape[1]
    vrows = table_master.shape[0]
    per_half = shards // tensor
    sub = vrows // groups
    esize = width * half

    ex = expert_change[0].reshape(mats, esize)
    tx = table_change[0].reshape(width, per_half, groups, sub)
    tx = jnp.transpose(tx, (2, 0, 1, 3)).reshape(groups, -1)
    q = rep_scatter((ex, tx))

    other = lax.ppermute(q, "tp", pairs(tensor, 1))
    halves = jax.tree.map(
        lambda a, b: jnp.where(t == 0, jnp.stack([a, b]), jnp.stack([b, a])), q, other
    )
    he = halves[0].reshape(tensor, width, per_half, rows)
    he = jnp.transpose(he, (0, 2, 1, 3)).reshape(shards, width * rows)
    ht = halves[1].reshape(tensor, width, per_half, sub)
    ht = jnp.transpose(ht, (0, 2, 1, 3)).reshape(shards, width * sub)
    got = lax.all_to_all(jnp.concatenate([he, ht], 1), "shard", 0, 0, tiled=True)

    ge = got[:, : width * rows].reshape(shards, width, rows)
    gt = got[:, width * rows :].reshape(shards, width, sub)

    r = lax.axis_index("rep")
    own_e = jnp.transpose(ge.reshape(shards * width, rows)) / groups
    own_e, _ = update(
        lax.dynamic_index_in_dim(expert_master, r, 0, keepdims=False),
        lax.dynamic_index_in_dim(expert_moment, r, 0, keepdims=False),
        own_e,
    )
    le = jnp.transpose(own_e.astype(jnp.bfloat16).reshape(rows, shards, width), (1, 2, 0))
    own_t = jnp.transpose(gt.reshape(shards * width, sub)) / groups
    own_t, _ = update(
        lax.dynamic_slice_in_dim(table_master, r * sub, sub, 0),
        lax.dynamic_slice_in_dim(table_moment, r * sub, sub, 0),
        own_t,
    )
    lt = jnp.transpose(own_t.astype(jnp.bfloat16).reshape(sub, shards, width), (1, 2, 0))
    back = jnp.concatenate([le.reshape(shards, -1), lt.reshape(shards, -1)], 1)
    back = lax.all_to_all(back, "shard", 0, 0, tiled=True)

    pieces_e = gather_pieces(ge)
    n_rep = lax.axis_size("rep")
    sib_t = lax.ppermute(gt, "rep", pairs(n_rep, 1))
    gt_late, _ = lax.optimization_barrier((gt, pieces_e[2]))
    cross_t = lax.ppermute(gt_late, "rep", pairs(n_rep, 2))
    sib_cross_t = lax.ppermute(cross_t, "rep", pairs(n_rep, 1))
    scale = 1.0 / groups
    early_t = fused_update((gt, sib_t), 0, table_master, table_moment, scale)
    pieces_e, early_t = lax.optimization_barrier((pieces_e, early_t))
    expert_weights, expert_velocity = fused_update(
        pieces_e, 0, expert_master, expert_moment, scale
    )

    back = lax.dynamic_slice_in_dim(back, t * per_half, per_half, 0)
    allq = rep_gather(back)
    ce = allq[:, :, : width * rows].reshape(groups, per_half, width, rows)
    expert_copies = jnp.transpose(ce, (0, 2, 1, 3)).reshape(mats, width, per_half * rows)
    ct = allq[:, :, width * rows :].reshape(groups, per_half, width, sub)
    table_copies = jnp.transpose(ct, (2, 1, 0, 3)).reshape(width, per_half * vrows)
    late, expert_copies, table_copies = lax.optimization_barrier(
        ((cross_t, sib_cross_t), expert_copies, table_copies)
    )
    table_weights, table_velocity = fused_update(
        late, 2, table_master, table_moment, scale, early_t
    )
    return (
        expert_weights,
        expert_velocity,
        expert_copies,
        table_weights,
        table_velocity,
        table_copies,
    )


def solution(mesh):
    in_specs = (
        P("rep", None, "shard", "tp"),
        P("rep", "shard", "tp"),
        P(None, "shard", None),
        P(None, "shard", None),
        P("shard", None),
        P("shard", None),
    )
    out_specs = (
        P(None, "shard", None),
        P(None, "shard", None),
        P(None, "shard", "tp"),
        P("shard", None),
        P("shard", None),
        P("shard", "tp"),
    )
    return jax.shard_map(local, mesh=mesh, in_specs=in_specs, out_specs=out_specs, check_vma=False)
```

```python
import jax
import jax.numpy as jnp
from jax import lax
from jax.sharding import PartitionSpec as P
from jax.experimental import pallas as pl
from jax.experimental.pallas import tpu as pltpu

momentum_coef = 0.9
outer_rate = 0.7


def update(master, moment, mean):
    velocity = momentum_coef * moment + mean
    weights = master - outer_rate * (mean + momentum_coef * velocity)
    return weights, velocity


def pairs(n, flip):
    return [(i, i ^ flip) for i in range(n)]


def rep_scatter(x):
    r = lax.axis_index("rep")
    n = lax.axis_size("rep")
    core, x_lo = r % 2, r // 2
    x4 = jax.tree.map(lambda a: a.reshape(2, 2, -1), x)
    pick = lambda tree, i, axis: jax.tree.map(
        lambda a: lax.dynamic_index_in_dim(a, i, axis, keepdims=False), tree
    )
    got = lax.ppermute(pick(x4, 1 - core, 1), "rep", pairs(n, 1))
    a = jax.tree.map(jnp.add, pick(x4, core, 1), got)
    got = lax.ppermute(pick(a, 1 - x_lo, 0), "rep", pairs(n, 2))
    return jax.tree.map(jnp.add, pick(a, x_lo, 0), got)


def rep_gather(x):
    r = lax.axis_index("rep")
    n = lax.axis_size("rep")
    core, x_lo = r % 2, r // 2
    cross = lax.ppermute(x, "rep", pairs(n, 2))
    pair = jax.tree.map(
        lambda a, b: jnp.where(x_lo == 0, jnp.stack([a, b]), jnp.stack([b, a])), x, cross
    )
    sib = lax.ppermute(pair, "rep", pairs(n, 1))
    full = jax.tree.map(
        lambda a, b: jnp.where(core == 0, jnp.stack([a, b], 1), jnp.stack([b, a], 1)), pair, sib
    )
    return jax.tree.map(lambda a, f: f.reshape((n,) + a.shape), x, full)


def gather_pieces(x):
    r = lax.axis_index("rep")
    n = lax.axis_size("rep")
    sib = lax.ppermute(x, "rep", pairs(n, 1))
    cross = lax.ppermute(x, "rep", pairs(n, 2))
    sib_cross = lax.ppermute(cross, "rep", pairs(n, 1))
    return x, sib, cross, sib_cross


def update_kernel(scale, count, r_ref, *refs):
    pieces = refs[:count]
    master_ref, moment_ref = refs[count : count + 2]
    w_ref, v_ref = refs[-2:]
    p = pl.program_id(0)
    for i, piece in enumerate(pieces):

        @pl.when(p == i)
        def _():
            x = piece[...]
            x = x.reshape(x.shape[0] * x.shape[1], x.shape[2])
            mean = x.T * scale
            weights, velocity = update(
                master_ref[...], moment_ref[...], mean.reshape(master_ref.shape)
            )
            w_ref[...] = weights
            v_ref[...] = velocity


def fused_update(pieces, first, master, moment, scale, into=None):
    srcs, wdt, cols = pieces[0].shape
    count = len(pieces)
    lead = master.shape[:-2]
    if lead:
        blk = (1,) * len(lead) + master.shape[-2:]
        idx = lambda p, r_ref: (lax.bitwise_xor(r_ref[0], p + first), 0, 0)
    else:
        blk = (cols,) + master.shape[-1:]
        idx = lambda p, r_ref: (lax.bitwise_xor(r_ref[0], p + first), 0)
    big = pl.BlockSpec(blk, idx)
    whole = pl.BlockSpec((srcs, wdt, cols), lambda p, r_ref: (0, 0, 0))
    r = lax.axis_index("rep").astype(jnp.int32).reshape(1)
    args = [r, *pieces, master, moment]
    in_specs = [whole] * count + [big, big]
    aliases = {}
    if into is not None:
        aliases = {len(args): 0, len(args) + 1: 1}
        args += list(into)
        in_specs += [pl.BlockSpec(memory_space=pl.ANY)] * 2
    return pl.pallas_call(
        lambda *refs: update_kernel(scale, count, *refs),
        grid_spec=pltpu.PrefetchScalarGridSpec(
            num_scalar_prefetch=1,
            grid=(count,),
            in_specs=in_specs,
            out_specs=[big, big],
        ),
        out_shape=[
            jax.ShapeDtypeStruct(master.shape, master.dtype),
            jax.ShapeDtypeStruct(master.shape, master.dtype),
        ],
        input_output_aliases=aliases,
    )(*args)


def local(expert_change, table_change, expert_master, expert_moment, table_master, table_moment):
    groups = lax.axis_size("rep")
    tensor = lax.axis_size("tp")
    shards = lax.axis_size("shard")
    t = lax.axis_index("tp")
    mats, width, half = expert_change.shape[1:]
    rows = expert_master.shape[1]
    vrows = table_master.shape[0]
    per_half = shards // tensor
    sub = vrows // groups
    esize = width * half

    ex = expert_change[0].reshape(mats, esize)
    tx = table_change[0].reshape(width, per_half, groups, sub)
    tx = jnp.transpose(tx, (2, 0, 1, 3)).reshape(groups, -1)
    q = rep_scatter((ex, tx))

    other = lax.ppermute(q, "tp", pairs(tensor, 1))
    halves = jax.tree.map(
        lambda a, b: jnp.where(t == 0, jnp.stack([a, b]), jnp.stack([b, a])), q, other
    )
    he = halves[0].reshape(tensor, width, per_half, rows)
    he = jnp.transpose(he, (0, 2, 1, 3)).reshape(shards, width * rows)
    ht = halves[1].reshape(tensor, width, per_half, sub)
    ht = jnp.transpose(ht, (0, 2, 1, 3)).reshape(shards, width * sub)
    got = lax.all_to_all(jnp.concatenate([he, ht], 1), "shard", 0, 0, tiled=True)

    ge = got[:, : width * rows].reshape(shards, width, rows)
    gt = got[:, width * rows :].reshape(shards, width, sub)

    r = lax.axis_index("rep")
    own_e = jnp.transpose(ge.reshape(shards * width, rows)) / groups
    own_e, _ = update(
        lax.dynamic_index_in_dim(expert_master, r, 0, keepdims=False),
        lax.dynamic_index_in_dim(expert_moment, r, 0, keepdims=False),
        own_e,
    )
    le = jnp.transpose(own_e.astype(jnp.bfloat16).reshape(rows, shards, width), (1, 2, 0))
    own_t = jnp.transpose(gt.reshape(shards * width, sub)) / groups
    own_t, _ = update(
        lax.dynamic_slice_in_dim(table_master, r * sub, sub, 0),
        lax.dynamic_slice_in_dim(table_moment, r * sub, sub, 0),
        own_t,
    )
    lt = jnp.transpose(own_t.astype(jnp.bfloat16).reshape(sub, shards, width), (1, 2, 0))
    back = jnp.concatenate([le.reshape(shards, -1), lt.reshape(shards, -1)], 1)
    back = lax.all_to_all(back, "shard", 0, 0, tiled=True)

    pieces_e = gather_pieces(ge)
    n_rep = lax.axis_size("rep")
    sib_t = lax.ppermute(gt, "rep", pairs(n_rep, 1))
    gt_late, _ = lax.optimization_barrier((gt, pieces_e[2]))
    cross_t = lax.ppermute(gt_late, "rep", pairs(n_rep, 2))
    sib_cross_t = lax.ppermute(cross_t, "rep", pairs(n_rep, 1))
    scale = 1.0 / groups
    early_t = fused_update((gt, sib_t), 0, table_master, table_moment, scale)
    pieces_e, early_t = lax.optimization_barrier((pieces_e, early_t))
    expert_weights, expert_velocity = fused_update(
        pieces_e, 0, expert_master, expert_moment, scale
    )

    back, early_t = lax.optimization_barrier((back, early_t))
    back = lax.dynamic_slice_in_dim(back, t * per_half, per_half, 0)
    table_weights, table_velocity = fused_update(
        (cross_t, sib_cross_t), 2, table_master, table_moment, scale, early_t
    )
    allq = rep_gather(back)
    ce = allq[:, :, : width * rows].reshape(groups, per_half, width, rows)
    expert_copies = jnp.transpose(ce, (0, 2, 1, 3)).reshape(mats, width, per_half * rows)
    ct = allq[:, :, width * rows :].reshape(groups, per_half, width, sub)
    table_copies = jnp.transpose(ct, (2, 1, 0, 3)).reshape(width, per_half * vrows)
    return (
        expert_weights,
        expert_velocity,
        expert_copies,
        table_weights,
        table_velocity,
        table_copies,
    )


def solution(mesh):
    in_specs = (
        P("rep", None, "shard", "tp"),
        P("rep", "shard", "tp"),
        P(None, "shard", None),
        P(None, "shard", None),
        P("shard", None),
        P("shard", None),
    )
    out_specs = (
        P(None, "shard", None),
        P(None, "shard", None),
        P(None, "shard", "tp"),
        P("shard", None),
        P("shard", None),
        P("shard", "tp"),
    )
    return jax.shard_map(local, mesh=mesh, in_specs=in_specs, out_specs=out_specs, check_vma=False)
```

```python
import jax
import jax.numpy as jnp
from jax import lax
from jax.sharding import PartitionSpec as P
from jax.experimental import pallas as pl
from jax.experimental.pallas import tpu as pltpu

momentum_coef = 0.9
outer_rate = 0.7


def update(master, moment, mean):
    velocity = momentum_coef * moment + mean
    weights = master - outer_rate * (mean + momentum_coef * velocity)
    return weights, velocity


def pairs(n, flip):
    return [(i, i ^ flip) for i in range(n)]


def rep_scatter(x):
    r = lax.axis_index("rep")
    n = lax.axis_size("rep")
    core, x_lo = r % 2, r // 2
    x4 = jax.tree.map(lambda a: a.reshape(2, 2, -1), x)
    pick = lambda tree, i, axis: jax.tree.map(
        lambda a: lax.dynamic_index_in_dim(a, i, axis, keepdims=False), tree
    )
    got = lax.ppermute(pick(x4, 1 - core, 1), "rep", pairs(n, 1))
    a = jax.tree.map(jnp.add, pick(x4, core, 1), got)
    got = lax.ppermute(pick(a, 1 - x_lo, 0), "rep", pairs(n, 2))
    return jax.tree.map(jnp.add, pick(a, x_lo, 0), got)


def rep_gather(x):
    r = lax.axis_index("rep")
    n = lax.axis_size("rep")
    core, x_lo = r % 2, r // 2
    cross = lax.ppermute(x, "rep", pairs(n, 2))
    pair = jax.tree.map(
        lambda a, b: jnp.where(x_lo == 0, jnp.stack([a, b]), jnp.stack([b, a])), x, cross
    )
    sib = lax.ppermute(pair, "rep", pairs(n, 1))
    full = jax.tree.map(
        lambda a, b: jnp.where(core == 0, jnp.stack([a, b], 1), jnp.stack([b, a], 1)), pair, sib
    )
    return jax.tree.map(lambda a, f: f.reshape((n,) + a.shape), x, full)


def gather_pieces(x):
    r = lax.axis_index("rep")
    n = lax.axis_size("rep")
    sib = lax.ppermute(x, "rep", pairs(n, 1))
    cross = lax.ppermute(x, "rep", pairs(n, 2))
    sib_cross = lax.ppermute(cross, "rep", pairs(n, 1))
    return x, sib, cross, sib_cross


def update_kernel(scale, count, r_ref, *refs):
    pieces = refs[:count]
    master_ref, moment_ref = refs[count : count + 2]
    w_ref, v_ref = refs[-2:]
    p = pl.program_id(0)
    for i, piece in enumerate(pieces):

        @pl.when(p == i)
        def _():
            x = piece[...]
            x = x.reshape(x.shape[0] * x.shape[1], x.shape[2])
            mean = x.T * scale
            weights, velocity = update(
                master_ref[...], moment_ref[...], mean.reshape(master_ref.shape)
            )
            w_ref[...] = weights
            v_ref[...] = velocity


def fused_update(pieces, first, master, moment, scale, into=None):
    srcs, wdt, cols = pieces[0].shape
    count = len(pieces)
    lead = master.shape[:-2]
    if lead:
        blk = (1,) * len(lead) + master.shape[-2:]
        idx = lambda p, r_ref: (lax.bitwise_xor(r_ref[0], p + first), 0, 0)
    else:
        blk = (cols,) + master.shape[-1:]
        idx = lambda p, r_ref: (lax.bitwise_xor(r_ref[0], p + first), 0)
    big = pl.BlockSpec(blk, idx)
    whole = pl.BlockSpec((srcs, wdt, cols), lambda p, r_ref: (0, 0, 0))
    r = lax.axis_index("rep").astype(jnp.int32).reshape(1)
    args = [r, *pieces, master, moment]
    in_specs = [whole] * count + [big, big]
    aliases = {}
    if into is not None:
        aliases = {len(args): 0, len(args) + 1: 1}
        args += list(into)
        in_specs += [pl.BlockSpec(memory_space=pl.ANY)] * 2
    return pl.pallas_call(
        lambda *refs: update_kernel(scale, count, *refs),
        grid_spec=pltpu.PrefetchScalarGridSpec(
            num_scalar_prefetch=1,
            grid=(count,),
            in_specs=in_specs,
            out_specs=[big, big],
        ),
        out_shape=[
            jax.ShapeDtypeStruct(master.shape, master.dtype),
            jax.ShapeDtypeStruct(master.shape, master.dtype),
        ],
        input_output_aliases=aliases,
    )(*args)


def local(expert_change, table_change, expert_master, expert_moment, table_master, table_moment):
    groups = lax.axis_size("rep")
    tensor = lax.axis_size("tp")
    shards = lax.axis_size("shard")
    t = lax.axis_index("tp")
    mats, width, half = expert_change.shape[1:]
    rows = expert_master.shape[1]
    vrows = table_master.shape[0]
    per_half = shards // tensor
    sub = vrows // groups
    esize = width * half

    ex = expert_change[0].reshape(mats, esize)
    tx = table_change[0].reshape(width, per_half, groups, sub)
    tx = jnp.transpose(tx, (2, 0, 1, 3)).reshape(groups, -1)
    q = rep_scatter((ex, tx))

    other = lax.ppermute(q, "tp", pairs(tensor, 1))
    halves = jax.tree.map(
        lambda a, b: jnp.where(t == 0, jnp.stack([a, b]), jnp.stack([b, a])), q, other
    )
    he = halves[0].reshape(tensor, width, per_half, rows)
    he = jnp.transpose(he, (0, 2, 1, 3)).reshape(shards, width * rows)
    ht = halves[1].reshape(tensor, width, per_half, sub)
    ht = jnp.transpose(ht, (0, 2, 1, 3)).reshape(shards, width * sub)
    got = lax.all_to_all(jnp.concatenate([he, ht], 1), "shard", 0, 0, tiled=True)

    ge = got[:, : width * rows].reshape(shards, width, rows)
    gt = got[:, width * rows :].reshape(shards, width, sub)

    r = lax.axis_index("rep")
    own_e = jnp.transpose(ge.reshape(shards * width, rows)) / groups
    own_e, _ = update(
        lax.dynamic_index_in_dim(expert_master, r, 0, keepdims=False),
        lax.dynamic_index_in_dim(expert_moment, r, 0, keepdims=False),
        own_e,
    )
    le = jnp.transpose(own_e.astype(jnp.bfloat16).reshape(rows, shards, width), (1, 2, 0))
    own_t = jnp.transpose(gt.reshape(shards * width, sub)) / groups
    own_t, _ = update(
        lax.dynamic_slice_in_dim(table_master, r * sub, sub, 0),
        lax.dynamic_slice_in_dim(table_moment, r * sub, sub, 0),
        own_t,
    )
    lt = jnp.transpose(own_t.astype(jnp.bfloat16).reshape(sub, shards, width), (1, 2, 0))
    back = jnp.concatenate([le.reshape(shards, -1), lt.reshape(shards, -1)], 1)
    back = lax.all_to_all(back, "shard", 0, 0, tiled=True)

    pieces_e = gather_pieces(ge)
    n_rep = lax.axis_size("rep")
    sib_t = lax.ppermute(gt, "rep", pairs(n_rep, 1))
    gt_late, _ = lax.optimization_barrier((gt, pieces_e[2]))
    cross_t = lax.ppermute(gt_late, "rep", pairs(n_rep, 2))
    sib_cross_t = lax.ppermute(cross_t, "rep", pairs(n_rep, 1))
    scale = 1.0 / groups
    early_t = fused_update((gt, sib_t), 0, table_master, table_moment, scale)
    pieces_e, early_t = lax.optimization_barrier((pieces_e, early_t))
    expert_weights, expert_velocity = fused_update(
        pieces_e, 0, expert_master, expert_moment, scale
    )
    mid_t = fused_update((cross_t,), 2, table_master, table_moment, scale, early_t)
    table_weights, table_velocity = fused_update(
        (sib_cross_t,), 3, table_master, table_moment, scale, mid_t
    )

    back = lax.dynamic_slice_in_dim(back, t * per_half, per_half, 0)
    allq = rep_gather(back)
    ce = allq[:, :, : width * rows].reshape(groups, per_half, width, rows)
    expert_copies = jnp.transpose(ce, (0, 2, 1, 3)).reshape(mats, width, per_half * rows)
    ct = allq[:, :, width * rows :].reshape(groups, per_half, width, sub)
    table_copies = jnp.transpose(ct, (2, 1, 0, 3)).reshape(width, per_half * vrows)
    return (
        expert_weights,
        expert_velocity,
        expert_copies,
        table_weights,
        table_velocity,
        table_copies,
    )


def solution(mesh):
    in_specs = (
        P("rep", None, "shard", "tp"),
        P("rep", "shard", "tp"),
        P(None, "shard", None),
        P(None, "shard", None),
        P("shard", None),
        P("shard", None),
    )
    out_specs = (
        P(None, "shard", None),
        P(None, "shard", None),
        P(None, "shard", "tp"),
        P("shard", None),
        P("shard", None),
        P("shard", "tp"),
    )
    return jax.shard_map(local, mesh=mesh, in_specs=in_specs, out_specs=out_specs, check_vma=False)
```

```python
import jax
import jax.numpy as jnp
from jax import lax
from jax.sharding import PartitionSpec as P
from jax.experimental import pallas as pl
from jax.experimental.pallas import tpu as pltpu

momentum_coef = 0.9
outer_rate = 0.7


def update(master, moment, mean):
    velocity = momentum_coef * moment + mean
    weights = master - outer_rate * (mean + momentum_coef * velocity)
    return weights, velocity


def pairs(n, flip):
    return [(i, i ^ flip) for i in range(n)]


def rep_scatter(x):
    r = lax.axis_index("rep")
    n = lax.axis_size("rep")
    core, x_lo = r % 2, r // 2
    x4 = jax.tree.map(lambda a: a.reshape(2, 2, -1), x)
    pick = lambda tree, i, axis: jax.tree.map(
        lambda a: lax.dynamic_index_in_dim(a, i, axis, keepdims=False), tree
    )
    got = lax.ppermute(pick(x4, 1 - core, 1), "rep", pairs(n, 1))
    a = jax.tree.map(jnp.add, pick(x4, core, 1), got)
    got = lax.ppermute(pick(a, 1 - x_lo, 0), "rep", pairs(n, 2))
    return jax.tree.map(jnp.add, pick(a, x_lo, 0), got)


def rep_gather(x):
    r = lax.axis_index("rep")
    n = lax.axis_size("rep")
    core, x_lo = r % 2, r // 2
    cross = lax.ppermute(x, "rep", pairs(n, 2))
    pair = jax.tree.map(
        lambda a, b: jnp.where(x_lo == 0, jnp.stack([a, b]), jnp.stack([b, a])), x, cross
    )
    sib = lax.ppermute(pair, "rep", pairs(n, 1))
    full = jax.tree.map(
        lambda a, b: jnp.where(core == 0, jnp.stack([a, b], 1), jnp.stack([b, a], 1)), pair, sib
    )
    return jax.tree.map(lambda a, f: f.reshape((n,) + a.shape), x, full)


def gather_pieces(x):
    r = lax.axis_index("rep")
    n = lax.axis_size("rep")
    sib = lax.ppermute(x, "rep", pairs(n, 1))
    cross = lax.ppermute(x, "rep", pairs(n, 2))
    sib_cross = lax.ppermute(cross, "rep", pairs(n, 1))
    return x, sib, cross, sib_cross


def update_kernel(scale, count, r_ref, *refs):
    pieces = refs[:count]
    master_ref, moment_ref = refs[count : count + 2]
    w_ref, v_ref = refs[-2:]
    p = pl.program_id(0)
    for i, piece in enumerate(pieces):

        @pl.when(p == i)
        def _():
            x = piece[...]
            x = x.reshape(x.shape[0] * x.shape[1], x.shape[2])
            mean = x.T * scale
            weights, velocity = update(
                master_ref[...], moment_ref[...], mean.reshape(master_ref.shape)
            )
            w_ref[...] = weights
            v_ref[...] = velocity


def fused_update(pieces, first, master, moment, scale, into=None):
    srcs, wdt, cols = pieces[0].shape
    count = len(pieces)
    lead = master.shape[:-2]
    if lead:
        blk = (1,) * len(lead) + master.shape[-2:]
        idx = lambda p, r_ref: (lax.bitwise_xor(r_ref[0], p + first), 0, 0)
    else:
        blk = (cols,) + master.shape[-1:]
        idx = lambda p, r_ref: (lax.bitwise_xor(r_ref[0], p + first), 0)
    big = pl.BlockSpec(blk, idx)
    whole = pl.BlockSpec((srcs, wdt, cols), lambda p, r_ref: (0, 0, 0))
    r = lax.axis_index("rep").astype(jnp.int32).reshape(1)
    args = [r, *pieces, master, moment]
    in_specs = [whole] * count + [big, big]
    aliases = {}
    if into is not None:
        aliases = {len(args): 0, len(args) + 1: 1}
        args += list(into)
        in_specs += [pl.BlockSpec(memory_space=pl.ANY)] * 2
    return pl.pallas_call(
        lambda *refs: update_kernel(scale, count, *refs),
        grid_spec=pltpu.PrefetchScalarGridSpec(
            num_scalar_prefetch=1,
            grid=(count,),
            in_specs=in_specs,
            out_specs=[big, big],
        ),
        out_shape=[
            jax.ShapeDtypeStruct(master.shape, master.dtype),
            jax.ShapeDtypeStruct(master.shape, master.dtype),
        ],
        input_output_aliases=aliases,
    )(*args)


def local(expert_change, table_change, expert_master, expert_moment, table_master, table_moment):
    groups = lax.axis_size("rep")
    tensor = lax.axis_size("tp")
    shards = lax.axis_size("shard")
    t = lax.axis_index("tp")
    mats, width, half = expert_change.shape[1:]
    rows = expert_master.shape[1]
    vrows = table_master.shape[0]
    per_half = shards // tensor
    sub = vrows // groups
    esize = width * half

    ex = expert_change[0].reshape(mats, esize)
    tx = table_change[0].reshape(width, per_half, groups, sub)
    tx = jnp.transpose(tx, (2, 0, 1, 3)).reshape(groups, -1)
    q = rep_scatter((ex, tx))

    other = lax.ppermute(q, "tp", pairs(tensor, 1))
    halves = jax.tree.map(
        lambda a, b: jnp.where(t == 0, jnp.stack([a, b]), jnp.stack([b, a])), q, other
    )
    he = halves[0].reshape(tensor, width, per_half, rows)
    he = jnp.transpose(he, (0, 2, 1, 3)).reshape(shards, width * rows)
    ht = halves[1].reshape(tensor, width, per_half, sub)
    ht = jnp.transpose(ht, (0, 2, 1, 3)).reshape(shards, width * sub)
    got = lax.all_to_all(jnp.concatenate([he, ht], 1), "shard", 0, 0, tiled=True)

    ge = got[:, : width * rows].reshape(shards, width, rows)
    gt = got[:, width * rows :].reshape(shards, width, sub)

    r = lax.axis_index("rep")
    own_e = jnp.transpose(ge.reshape(shards * width, rows)) / groups
    own_e, _ = update(
        lax.dynamic_index_in_dim(expert_master, r, 0, keepdims=False),
        lax.dynamic_index_in_dim(expert_moment, r, 0, keepdims=False),
        own_e,
    )
    le = jnp.transpose(own_e.astype(jnp.bfloat16).reshape(rows, shards, width), (1, 2, 0))
    own_t = jnp.transpose(gt.reshape(shards * width, sub)) / groups
    own_t, _ = update(
        lax.dynamic_slice_in_dim(table_master, r * sub, sub, 0),
        lax.dynamic_slice_in_dim(table_moment, r * sub, sub, 0),
        own_t,
    )
    lt = jnp.transpose(own_t.astype(jnp.bfloat16).reshape(sub, shards, width), (1, 2, 0))
    back = jnp.concatenate([le.reshape(shards, -1), lt.reshape(shards, -1)], 1)
    back = lax.all_to_all(back.reshape(shards, 2, -1), "shard", 0, 0, tiled=True)
    back = back.reshape(shards, -1)

    pieces_e = gather_pieces(ge)
    n_rep = lax.axis_size("rep")
    sib_t = lax.ppermute(gt, "rep", pairs(n_rep, 1))
    gt_late, _ = lax.optimization_barrier((gt, pieces_e[2]))
    cross_t = lax.ppermute(gt_late, "rep", pairs(n_rep, 2))
    sib_cross_t = lax.ppermute(cross_t, "rep", pairs(n_rep, 1))
    scale = 1.0 / groups
    early_t = fused_update((gt, sib_t), 0, table_master, table_moment, scale)
    pieces_e, early_t = lax.optimization_barrier((pieces_e, early_t))
    expert_weights, expert_velocity = fused_update(
        pieces_e, 0, expert_master, expert_moment, scale
    )
    table_weights, table_velocity = fused_update(
        (cross_t, sib_cross_t), 2, table_master, table_moment, scale, early_t
    )

    back = lax.dynamic_slice_in_dim(back, t * per_half, per_half, 0)
    allq = rep_gather(back)
    ce = allq[:, :, : width * rows].reshape(groups, per_half, width, rows)
    expert_copies = jnp.transpose(ce, (0, 2, 1, 3)).reshape(mats, width, per_half * rows)
    ct = allq[:, :, width * rows :].reshape(groups, per_half, width, sub)
    table_copies = jnp.transpose(ct, (2, 1, 0, 3)).reshape(width, per_half * vrows)
    return (
        expert_weights,
        expert_velocity,
        expert_copies,
        table_weights,
        table_velocity,
        table_copies,
    )


def solution(mesh):
    in_specs = (
        P("rep", None, "shard", "tp"),
        P("rep", "shard", "tp"),
        P(None, "shard", None),
        P(None, "shard", None),
        P("shard", None),
        P("shard", None),
    )
    out_specs = (
        P(None, "shard", None),
        P(None, "shard", None),
        P(None, "shard", "tp"),
        P("shard", None),
        P("shard", None),
        P("shard", "tp"),
    )
    return jax.shard_map(local, mesh=mesh, in_specs=in_specs, out_specs=out_specs, check_vma=False)
```

```python
import jax
import jax.numpy as jnp
from jax import lax
from jax.sharding import PartitionSpec as P
from jax.experimental import pallas as pl
from jax.experimental.pallas import tpu as pltpu

momentum_coef = 0.9
outer_rate = 0.7


def update(master, moment, mean):
    velocity = momentum_coef * moment + mean
    weights = master - outer_rate * (mean + momentum_coef * velocity)
    return weights, velocity


def pairs(n, flip):
    return [(i, i ^ flip) for i in range(n)]


def rep_scatter(x):
    r = lax.axis_index("rep")
    n = lax.axis_size("rep")
    core, x_lo = r % 2, r // 2
    x4 = jax.tree.map(lambda a: a.reshape(2, 2, -1), x)
    pick = lambda tree, i, axis: jax.tree.map(
        lambda a: lax.dynamic_index_in_dim(a, i, axis, keepdims=False), tree
    )
    got = lax.ppermute(pick(x4, 1 - core, 1), "rep", pairs(n, 1))
    a = jax.tree.map(jnp.add, pick(x4, core, 1), got)
    got = lax.ppermute(pick(a, 1 - x_lo, 0), "rep", pairs(n, 2))
    return jax.tree.map(jnp.add, pick(a, x_lo, 0), got)


def rep_gather(x):
    r = lax.axis_index("rep")
    n = lax.axis_size("rep")
    core, x_lo = r % 2, r // 2
    cross = lax.ppermute(x, "rep", pairs(n, 2))
    pair = jax.tree.map(
        lambda a, b: jnp.where(x_lo == 0, jnp.stack([a, b]), jnp.stack([b, a])), x, cross
    )
    sib = lax.ppermute(pair, "rep", pairs(n, 1))
    full = jax.tree.map(
        lambda a, b: jnp.where(core == 0, jnp.stack([a, b], 1), jnp.stack([b, a], 1)), pair, sib
    )
    return jax.tree.map(lambda a, f: f.reshape((n,) + a.shape), x, full)


def gather_pieces(x):
    r = lax.axis_index("rep")
    n = lax.axis_size("rep")
    sib = lax.ppermute(x, "rep", pairs(n, 1))
    cross = lax.ppermute(x, "rep", pairs(n, 2))
    sib_cross = lax.ppermute(cross, "rep", pairs(n, 1))
    return x, sib, cross, sib_cross


def update_kernel(scale, count, r_ref, *refs):
    pieces = refs[:count]
    master_ref, moment_ref = refs[count : count + 2]
    w_ref, v_ref = refs[-2:]
    p = pl.program_id(0)
    for i, piece in enumerate(pieces):

        @pl.when(p == i)
        def _():
            x = piece[...]
            x = x.reshape(x.shape[0] * x.shape[1], x.shape[2])
            mean = x.T * scale
            weights, velocity = update(
                master_ref[...], moment_ref[...], mean.reshape(master_ref.shape)
            )
            w_ref[...] = weights
            v_ref[...] = velocity


def fused_update(pieces, first, master, moment, scale, into=None):
    srcs, wdt, cols = pieces[0].shape
    count = len(pieces)
    lead = master.shape[:-2]
    if lead:
        blk = (1,) * len(lead) + master.shape[-2:]
        idx = lambda p, r_ref: (lax.bitwise_xor(r_ref[0], p + first), 0, 0)
    else:
        blk = (cols,) + master.shape[-1:]
        idx = lambda p, r_ref: (lax.bitwise_xor(r_ref[0], p + first), 0)
    big = pl.BlockSpec(blk, idx)
    whole = pl.BlockSpec((srcs, wdt, cols), lambda p, r_ref: (0, 0, 0))
    r = lax.axis_index("rep").astype(jnp.int32).reshape(1)
    args = [r, *pieces, master, moment]
    in_specs = [whole] * count + [big, big]
    aliases = {}
    if into is not None:
        aliases = {len(args): 0, len(args) + 1: 1}
        args += list(into)
        in_specs += [pl.BlockSpec(memory_space=pl.ANY)] * 2
    return pl.pallas_call(
        lambda *refs: update_kernel(scale, count, *refs),
        grid_spec=pltpu.PrefetchScalarGridSpec(
            num_scalar_prefetch=1,
            grid=(count,),
            in_specs=in_specs,
            out_specs=[big, big],
        ),
        out_shape=[
            jax.ShapeDtypeStruct(master.shape, master.dtype),
            jax.ShapeDtypeStruct(master.shape, master.dtype),
        ],
        input_output_aliases=aliases,
    )(*args)


def local(expert_change, table_change, expert_master, expert_moment, table_master, table_moment):
    groups = lax.axis_size("rep")
    tensor = lax.axis_size("tp")
    shards = lax.axis_size("shard")
    t = lax.axis_index("tp")
    mats, width, half = expert_change.shape[1:]
    rows = expert_master.shape[1]
    vrows = table_master.shape[0]
    per_half = shards // tensor
    sub = vrows // groups
    esize = width * half

    ex = expert_change[0].reshape(mats, esize)
    tx = table_change[0].reshape(width, per_half, groups, sub)
    tx = jnp.transpose(tx, (2, 0, 1, 3)).reshape(groups, -1)
    q = rep_scatter((ex, tx))

    other = lax.ppermute(q, "tp", pairs(tensor, 1))
    halves = jax.tree.map(
        lambda a, b: jnp.where(t == 0, jnp.stack([a, b]), jnp.stack([b, a])), q, other
    )
    he = halves[0].reshape(tensor, width, per_half, rows)
    he = jnp.transpose(he, (0, 2, 1, 3)).reshape(shards, width * rows)
    ht = halves[1].reshape(tensor, width, per_half, sub)
    ht = jnp.transpose(ht, (0, 2, 1, 3)).reshape(shards, width * sub)
    got = lax.all_to_all(jnp.concatenate([he, ht], 1), "shard", 0, 0, tiled=True)

    ge = got[:, : width * rows].reshape(shards, width, rows)
    gt = got[:, width * rows :].reshape(shards, width, sub)

    r = lax.axis_index("rep")
    own_e = jnp.transpose(ge.reshape(shards * width, rows)) / groups
    own_e, _ = update(
        lax.dynamic_index_in_dim(expert_master, r, 0, keepdims=False),
        lax.dynamic_index_in_dim(expert_moment, r, 0, keepdims=False),
        own_e,
    )
    le = jnp.transpose(own_e.astype(jnp.bfloat16).reshape(rows, shards, width), (1, 2, 0))
    own_t = jnp.transpose(gt.reshape(shards * width, sub)) / groups
    own_t, _ = update(
        lax.dynamic_slice_in_dim(table_master, r * sub, sub, 0),
        lax.dynamic_slice_in_dim(table_moment, r * sub, sub, 0),
        own_t,
    )
    lt = jnp.transpose(own_t.astype(jnp.bfloat16).reshape(sub, shards, width), (1, 2, 0))
    back = jnp.concatenate([le.reshape(shards, -1), lt.reshape(shards, -1)], 1)
    back = lax.all_to_all(back.reshape(shards, 2, -1), "shard", 0, 0, tiled=True)
    back = back.reshape(shards, -1)

    pieces_e = gather_pieces(ge)
    n_rep = lax.axis_size("rep")
    sib_t = lax.ppermute(gt, "rep", pairs(n_rep, 1))
    gt_late, _ = lax.optimization_barrier((gt, pieces_e[2]))
    cross_t = lax.ppermute(gt_late, "rep", pairs(n_rep, 2))
    sib_cross_t = lax.ppermute(cross_t, "rep", pairs(n_rep, 1))
    scale = 1.0 / groups
    early_t = fused_update((gt, sib_t), 0, table_master, table_moment, scale)
    pieces_e, early_t = lax.optimization_barrier((pieces_e, early_t))
    expert_weights, expert_velocity = fused_update(
        pieces_e, 0, expert_master, expert_moment, scale
    )
    table_weights, table_velocity = fused_update(
        (cross_t, sib_cross_t), 2, table_master, table_moment, scale, early_t
    )

    back = lax.dynamic_slice_in_dim(back, t * per_half, per_half, 0)
    bp = gather_pieces(back)

    def quarter(q):
        pick = lambda p: (r ^ q) == p
        return jnp.where(
            pick(0), bp[0], jnp.where(pick(1), bp[1], jnp.where(pick(2), bp[2], bp[3]))
        )

    allq = jnp.stack([quarter(q) for q in range(groups)])
    ce = allq[:, :, : width * rows].reshape(groups, per_half, width, rows)
    expert_copies = jnp.transpose(ce, (0, 2, 1, 3)).reshape(mats, width, per_half * rows)
    ct = allq[:, :, width * rows :].reshape(groups, per_half, width, sub)
    table_copies = jnp.transpose(ct, (2, 1, 0, 3)).reshape(width, per_half * vrows)
    return (
        expert_weights,
        expert_velocity,
        expert_copies,
        table_weights,
        table_velocity,
        table_copies,
    )


def solution(mesh):
    in_specs = (
        P("rep", None, "shard", "tp"),
        P("rep", "shard", "tp"),
        P(None, "shard", None),
        P(None, "shard", None),
        P("shard", None),
        P("shard", None),
    )
    out_specs = (
        P(None, "shard", None),
        P(None, "shard", None),
        P(None, "shard", "tp"),
        P("shard", None),
        P("shard", None),
        P("shard", "tp"),
    )
    return jax.shard_map(local, mesh=mesh, in_specs=in_specs, out_specs=out_specs, check_vma=False)
```
